32 devices in a mesh: gx: 16 (over z, y, core), gy: 2 (over x).
Axes of the slice: x: 2, y: 2, z: 4, core: 2. Of those that a mesh axis runs over, the one named last changes fastest.
Arguments:
- tangent: bfloat16 [256, 1024, 256], P(None, 'gx', 'gy'), may hold values from -6 to 6
- courant_x: float32 [1024, 256], P('gx', 'gy'), may hold values from -0.5 to 0.5
- courant_y: float32 [1024, 256], P('gx', 'gy'), may hold values from -0.5 to 0.5
- growth: float32 [1024, 256], P('gx', 'gy'), may hold values from -0.15 to 0.15
Outputs:
- basis: bfloat16 [256, 1024, 256], P(None, 'gx', 'gy')
- factor: float32 [256, 256], replicated
- exponents: float32 [256], replicated
The draws below stay inside these ranges and needn't reach their ends.
All inputs are finite; a program needn't handle non-finite values.
Results may differ from the reference program's by a relative error of at most 0.001.
The reference program's roundings to bfloat16 on the way (of `evolved` and `inverse`) count: a program that leaves them out, or rounds other values in their place, can miss the bound.
Values may be sent and summed in bfloat16 or wider, within the bound.
No kernel may reach another device: no remote copies, remote signals or barrier semaphores. Data moves between devices by JAX's collectives and lax.ppermute only.
A program may use at most 128 MiB of HBM per device.

```python
import jax
import jax.numpy as jnp
from jax import lax

K = 256
SUBSTEPS = 4
NX = 1024
NY = 256


def block_levels(rng, dims, cuts, least, high):
    loudness, own = 1.0, jax.random.fold_in(rng, 6)
    for axis_at, shards_of in cuts:
        draws = jnp.exp(jax.random.uniform(jax.random.fold_in(own, axis_at), (shards_of,), jnp.float32, least / len(cuts), high / len(cuts)))
        loudness = loudness * jnp.repeat(draws, dims[axis_at] // shards_of).reshape([-1 if axis == axis_at else 1 for axis in range(len(dims))])
    return loudness


def noise(rng, shape, scale, limit, cuts=(), kind=jnp.bfloat16):
    level = block_levels(rng, shape, cuts, -0.22, 0.18) if cuts else 1.0
    array = jax.random.normal(rng, shape, jnp.float32) * scale * level
    return jnp.minimum(jnp.maximum(array, -limit), limit).astype(kind)


def setup_inputs(seed: int = 0) -> dict:
    streams_of = jax.random.split(jax.random.key(seed), 5)
    return {
        "tangent": noise(streams_of[0], (K, NX, NY), 1.0, 6.0, ((1, 16), (2, 2))),
        "courant_x": noise(streams_of[1], (NX, NY), 0.2, 0.5, ((0, 16), (1, 2)), jnp.float32),
        "courant_y": noise(streams_of[2], (NX, NY), 0.2, 0.5, ((0, 16), (1, 2)), jnp.float32),
        "growth": jnp.clip(jax.random.uniform(streams_of[3], (NX, NY), jnp.float32, -0.15, 0.15) * block_levels(streams_of[3], (NX, NY), ((0, 16), (1, 2)), -0.4, 0.0), -0.15, 0.15),
    }


def advance_block(block, courant_x, courant_y, growth):
    state = block.astype(jnp.float32)
    for step in range(SUBSTEPS):
        north = jnp.roll(state, -1, axis=1)
        south = jnp.roll(state, 1, axis=1)
        east = jnp.roll(state, -1, axis=2)
        west = jnp.roll(state, 1, axis=2)
        state = state + 0.2 * (north + south + east + west - 4.0 * state) - courant_x * (north - south) - courant_y * (east - west) + growth * state
    return state.astype(jnp.bfloat16)

def reference(tangent, courant_x, courant_y, growth):
    blocks = tangent.reshape(K // 16, 16, NX, NY)
    evolved = lax.map(lambda blk: advance_block(blk, courant_x, courant_y, growth), blocks)
    evolved = evolved.reshape(K, NX * NY)
    gram = jnp.dot(evolved.astype(jnp.float32), evolved.T.astype(jnp.float32), preferred_element_type=jnp.float32) / jnp.float32(NX * NY)
    lower = jnp.linalg.cholesky(gram)
    identity = jnp.eye(K, dtype=jnp.float32)
    inverse = lax.linalg.triangular_solve(lower, identity, left_side=True, lower=True).astype(jnp.bfloat16)
    basis = jnp.dot(inverse.astype(jnp.float32), evolved.astype(jnp.float32), preferred_element_type=jnp.float32)
    exponents = jnp.log(jnp.diagonal(lower))
    return (basis.astype(jnp.bfloat16).reshape(K, NX, NY), lower.T, exponents)
```

```python
import functools

import jax
import jax.numpy as jnp
from jax import lax
from jax.experimental import pallas as pl
from jax.experimental.pallas import tpu as pltpu
from jax.sharding import PartitionSpec as P

F32 = jnp.float32
BF16 = jnp.bfloat16
SUBSTEPS = 4
LANES = 128
HALO = SUBSTEPS
GROUP = 8
EDGE = 2 * HALO
PACKED = 16


def spread(row):
    return jnp.broadcast_to(row, (8, 128))

def factor_block(v):
    sub = lax.broadcasted_iota(jnp.int32, (8, 128), 0)
    n = 8
    for p in range(16):
        c0 = p * n
        diag = v[c0:c0 + n, 0:128]
        column = [jnp.broadcast_to(diag[:, c0 + j:c0 + j + 1], (n, 128)) for j in range(n)]
        d = {(i, j): spread(column[j][i:i + 1]) for j in range(n) for i in range(j + 1)}
        inv, r, x = {}, {}, {}
        for j in range(n):
            inv[j] = lax.rsqrt(d[j, j])
            for k in range(j + 1, n):
                r[j, k] = d[j, k] * inv[j]
            for i in range(j + 1, n):
                for k in range(i, n):
                    d[i, k] = d[i, k] - r[j, i] * r[j, k]
        for j in range(n):
            x[j, j] = inv[j]
            for i in range(j + 1, n):
                acc = r[j, i] * x[j, j]
                for k in range(j + 1, i):
                    acc = acc + r[k, i] * x[k, j]
                x[i, j] = -(inv[i] * acc)
        dinv = {}
        for a in range(n):
            for b in range(a, n):
                acc = x[b, a] * x[b, b]
                for m in range(b + 1, n):
                    acc = acc + x[m, a] * x[m, b]
                dinv[a, b] = dinv[b, a] = acc
        ys = []
        for t in range(3):
            cols = slice(128 * t, 128 * t + 128)
            rows = [spread(v[c0 + k:c0 + k + 1, cols]) for k in range(n)]
            ys.append([sum(dinv[a, k] * rows[k] for k in range(n)) for a in range(n)])
            out = x[0, 0] * rows[0]
            for i in range(1, n):
                out = jnp.where(sub == i, sum(x[i, k] * rows[k] for k in range(i + 1)), out)
            v[c0:c0 + n, cols] = out
        for g in range(p + 1, 16):
            ag = v[n * g:n * g + n, 0:128]
            ab = [jnp.broadcast_to(ag[:, c0 + j:c0 + j + 1], (n, 128)) for j in range(n)]
            for t in range(3):
                cols = slice(128 * t, 128 * t + 128)
                acc = v[n * g:n * g + n, cols]
                for j in range(n):
                    acc = acc - ab[j] * ys[t][j]
                v[n * g:n * g + n, cols] = acc

def dot_t(a, b):
    return lax.dot_general(a, b, (((0,), (0,)), ((), ())), precision=lax.Precision.HIGHEST, preferred_element_type=F32)

def factor_kernel(total, pay, factor, inverse, exponents, v):
    h = 128
    ri = lax.broadcasted_iota(jnp.int32, (h, h), 0)
    ci = lax.broadcasted_iota(jnp.int32, (h, h), 1)
    eye = jnp.where(ri == ci, 1.0, 0.0).astype(F32)
    fold = pay[0:h, :] / total
    turned = fold.T
    diag0 = jnp.broadcast_to(pay[2 * h:2 * h + 1, :], (h, h)) / total
    v[:, 0:h] = jnp.where(ri == ci, diag0, jnp.where(ri < ci, turned, fold))
    v[:, h:2 * h] = pay[h:2 * h, :] / total
    v[:, 2 * h:3 * h] = eye
    rest = jnp.where(ri <= ci, fold, turned)
    factor_block(v)
    r00 = jnp.where(ri <= ci, v[:, 0:h], 0.0)
    r01 = v[:, h:2 * h]
    l00 = jnp.where(ri >= ci, v[:, 2 * h:3 * h], 0.0)
    factor[0:h, 0:h] = r00
    factor[0:h, h:2 * h] = r01
    inverse[0:h, 0:h] = l00.astype(jnp.bfloat16)
    inverse[0:h, h:2 * h] = jnp.zeros((h, h), jnp.bfloat16)
    exponents[:, 0:h] = jnp.log(jnp.sum(r00 * eye, axis=0, keepdims=True))
    v[:, 0:h] = rest - dot_t(r01, r01)
    v[:, h:2 * h] = -dot_t(r01, l00)
    v[:, 2 * h:3 * h] = eye
    factor_block(v)
    r11 = jnp.where(ri <= ci, v[:, 0:h], 0.0)
    factor[h:2 * h, 0:h] = jnp.zeros((h, h), F32)
    factor[h:2 * h, h:2 * h] = r11
    inverse[h:2 * h, 0:h] = v[:, h:2 * h].astype(jnp.bfloat16)
    inverse[h:2 * h, h:2 * h] = jnp.where(ri >= ci, v[:, 2 * h:3 * h], 0.0).astype(jnp.bfloat16)
    exponents[:, h:2 * h] = jnp.log(jnp.sum(r11 * eye, axis=0, keepdims=True))

def factorize(pay, total):
    return pl.pallas_call(
        functools.partial(factor_kernel, total),
        out_shape=(jax.ShapeDtypeStruct((256,256),F32), jax.ShapeDtypeStruct((256,256),jnp.bfloat16), jax.ShapeDtypeStruct((1,256),F32)),
        scratch_shapes=[pltpu.VMEM((128,384),F32)],
        compiler_params=pltpu.CompilerParams(vmem_limit_bytes=16<<20),
    )(pay)

def arrange_kernel(tangent, arranged, wide):
    fields, rows, lanes = tangent.shape
    block = lax.broadcasted_iota(jnp.int32, (PACKED, lanes), 1) // EDGE

    def spread_field(f, carry):
        values = tangent[f].astype(F32)
        for part in range(rows // GROUP):
            wide[pl.ds(f + fields * GROUP * part, GROUP, stride=fields), :] = values[GROUP * part:GROUP * (part + 1)]
        return carry

    lax.fori_loop(0, fields, spread_field, 0, unroll=8)

    def pack_row(r, carry):
        start = pl.multiple_of(r * fields, fields)
        arranged[r, 0:fields] = wide[pl.ds(start, fields), :].astype(BF16)
        edge = None
        for b in range(fields // PACKED):
            part = wide[pl.ds(start + PACKED * b, PACKED), :]
            moved = pltpu.roll(part, (EDGE * b + HALO) % lanes, 1)
            edge = moved if edge is None else jnp.where(block == b, moved, edge)
        arranged[r, fields:fields + PACKED] = edge.astype(BF16)
        return carry

    lax.fori_loop(0, rows, pack_row, 0)


def arrange(tangent):
    fields, rows, lanes = tangent.shape
    step = 16
    return pl.pallas_call(
        arrange_kernel,
        grid=(rows // step,),
        in_specs=[pl.BlockSpec((fields, step, lanes), lambda i: (0, i, 0))],
        out_specs=pl.BlockSpec((step, fields + PACKED, lanes), lambda i: (i, 0, 0)),
        out_shape=jax.ShapeDtypeStruct((rows, fields + PACKED, lanes), BF16),
        scratch_shapes=[pltpu.VMEM((step * fields, lanes), F32)],
        compiler_params=pltpu.CompilerParams(vmem_limit_bytes=32 << 20),
    )(tangent)


def evolve_kernel(own, low, high, west, east, low_west, low_east, high_west, high_east, inner, left, right,
                  evolved, payload, first, second, gram):
    rows, _, lanes = own.shape
    fields = own.shape[1] - PACKED
    lane = lax.broadcasted_iota(jnp.int32, (GROUP, lanes), 1)
    in_edge = lane % EDGE
    lane16 = lax.broadcasted_iota(jnp.int32, (PACKED, lanes), 1) % EDGE
    west_at, east_at = fields, fields + PACKED

    def fill(target, mine, from_west, from_east):
        first[target, 0:fields] = mine[0:fields].astype(F32)
        edge = mine[fields:fields + PACKED].astype(F32)
        first[target, west_at:west_at + PACKED] = jnp.where(lane16 < HALO, from_west.astype(F32), edge)
        first[target, east_at:east_at + PACKED] = jnp.where(lane16 < HALO, edge, from_east.astype(F32))

    for i in range(HALO):
        fill(i, low[i], low_west[i], low_east[i])
        fill(HALO + rows + i, high[i], high_west[i], high_east[i])

    def fill_own(r, carry):
        fill(HALO + r, own[r], west[r], east[r])
        return carry

    lax.fori_loop(0, rows, fill_own, 0)

    def coefficients(table, r):
        return [jnp.broadcast_to(table[m, pl.ds(r, 1)], (GROUP, lanes)) for m in range(5)]

    def combine(coef, c, n, s, e, w):
        return coef[0] * c + (coef[1] * n + coef[2] * s) + (coef[3] * e + coef[4] * w)

    def joints(source, r):
        out = []
        for h in range(PACKED // GROUP):
            from_west = source[r, west_at + GROUP * h:west_at + GROUP * (h + 1)]
            from_east = source[r, east_at + GROUP * h:east_at + GROUP * (h + 1)]
            out.append(jnp.where(in_edge == HALO - 1, from_west, pltpu.roll(from_east, lanes - 2, 1)))
        return out

    def interior(source, r, k, coef, joint):
        at = slice(GROUP * k, GROUP * (k + 1))
        b, h = divmod(k, PACKED // GROUP)
        beyond = pltpu.roll(joint[h], (lanes - (EDGE * b + HALO - 1)) % lanes, 1)
        c = source[r, at]
        e = jnp.where(lane == lanes - 1, beyond, pltpu.roll(c, lanes - 1, 1))
        w = jnp.where(lane == 0, beyond, pltpu.roll(c, 1, 1))
        return combine(coef, c, source[r + 1, at], source[r - 1, at], e, w)

    def substep(source, target, step):
        def row(r, carry):
            coef = coefficients(inner, r)
            joint = joints(source, r)
            for k in range(fields // GROUP):
                target[r, GROUP * k:GROUP * (k + 1)] = interior(source, r, k, coef, joint)
            for table, at in ((left, west_at), (right, east_at)):
                coef = coefficients(table, r)
                for h in range(PACKED // GROUP):
                    where = slice(at + GROUP * h, at + GROUP * (h + 1))
                    c = source[r, where]
                    target[r, where] = combine(
                        coef, c, source[r + 1, where], source[r - 1, where],
                        pltpu.roll(c, lanes - 1, 1), pltpu.roll(c, 1, 1))
            return carry

        lax.fori_loop(step, 2 * HALO + rows - step, row, 0)

    buffers = [first, second]
    for step in range(1, SUBSTEPS):
        substep(buffers[(step - 1) % 2], buffers[step % 2], step)
    source = buffers[(SUBSTEPS - 1) % 2]
    gram[...] = jnp.zeros_like(gram)
    chunk = 8

    def last_chunk(q, carry):
        def row(i, inner_carry):
            r = q * chunk + i
            coef = coefficients(inner, HALO + r)
            joint = joints(source, HALO + r)
            at = pl.multiple_of(r * lanes, lanes)
            for k in range(0, fields // GROUP, 2):
                pair = [interior(source, HALO + r, k + h, coef, joint) for h in range(2)]
                evolved[GROUP * k:GROUP * (k + 2), pl.ds(at, lanes)] = jnp.concatenate(pair, axis=0).astype(BF16)
            return inner_carry

        lax.fori_loop(0, chunk, row, 0)
        part = evolved[:, pl.ds(pl.multiple_of(q * chunk * lanes, chunk * lanes), chunk * lanes)]
        gram[...] += lax.dot_general(part, part, (((1,), (1,)), ((), ())), preferred_element_type=F32)
        return carry

    lax.fori_loop(0, rows // chunk, last_chunk, 0)
    h = fields // 2
    ri = lax.broadcasted_iota(jnp.int32, (h, h), 0)
    ci = lax.broadcasted_iota(jnp.int32, (h, h), 1)
    corner = gram[0:h, 0:h]
    payload[0:h] = jnp.where(ri <= ci, gram[h:2 * h, h:2 * h], corner)
    payload[h:2 * h] = gram[0:h, h:2 * h]
    diagonal = jnp.sum(jnp.where(ri == ci, corner, 0.0), axis=0, keepdims=True)
    payload[2 * h:] = jnp.broadcast_to(diagonal, (PACKED, h))


def evolve(own, halos, tables):
    rows, tall, lanes = own.shape
    fields = tall - PACKED
    extended = (rows + 2 * HALO, fields + 2 * PACKED, lanes)
    return pl.pallas_call(
        evolve_kernel,
        out_shape=(
            jax.ShapeDtypeStruct((fields, rows * lanes), BF16),
            jax.ShapeDtypeStruct((fields + PACKED, fields // 2), F32),
        ),
        scratch_shapes=[
            pltpu.VMEM(extended, F32),
            pltpu.VMEM(extended, F32),
            pltpu.VMEM((fields, fields), F32),
        ],
        compiler_params=pltpu.CompilerParams(vmem_limit_bytes=56 << 20),
    )(own, *halos, *tables)


def project_kernel(inverse, evolved, basis, wide):
    fields, rows, lanes = basis.shape
    for r in range(0, rows, 2):
        part = jnp.dot(inverse[...], evolved[:, r * lanes:(r + 2) * lanes], preferred_element_type=F32)
        for i in range(2):
            wide[pl.ds(r + i, fields, stride=rows), :] = part[:, i * lanes:(i + 1) * lanes]
    basis[...] = wide[...].reshape(fields, rows, lanes).astype(BF16)


def project(inverse, evolved, rows):
    fields, cells = evolved.shape
    lanes = cells // rows
    step = 16
    return pl.pallas_call(
        project_kernel,
        grid=(rows // step,),
        in_specs=[
            pl.BlockSpec((fields, fields), lambda i: (0, 0)),
            pl.BlockSpec((fields, step * lanes), lambda i: (0, i)),
        ],
        out_specs=pl.BlockSpec((fields, step, lanes), lambda i: (0, i, 0)),
        out_shape=jax.ShapeDtypeStruct((fields, rows, lanes), BF16),
        scratch_shapes=[pltpu.VMEM((step * fields, lanes), F32)],
        compiler_params=pltpu.CompilerParams(vmem_limit_bytes=32 << 20),
    )(inverse, evolved)


def shifted(block, down, right):
    nx, ny = lax.axis_size("gx"), lax.axis_size("gy")
    pairs = []
    for x in range(nx):
        for y in range(ny):
            pairs.append((x * ny + y, (x + down) % nx * ny + (y + right) % ny))
    return lax.ppermute(block, ("gx", "gy"), pairs)


def swapped(block, axis, bit):
    return lax.ppermute(block, axis, [(i, i ^ bit) for i in range(lax.axis_size(axis))])


def summed(payload):
    nx, ny = lax.axis_size("gx"), lax.axis_size("gy")
    if nx & (nx - 1) or ny & (ny - 1) or nx < 2:
        return lax.psum(payload, ("gx", "gy"))
    half = payload.shape[0] // 2
    side = lax.axis_index("gx") % 2
    kept = lax.dynamic_slice_in_dim(payload, side * half, half, 0)
    given = lax.dynamic_slice_in_dim(payload, (1 - side) * half, half, 0)
    total = kept + swapped(given, "gx", 1)
    for axis, bits in (("gy", range(ny.bit_length() - 1)), ("gx", range(1, nx.bit_length() - 1))):
        for bit in bits:
            total = total + swapped(total, axis, 1 << bit)
    other = swapped(total, "gx", 1)
    return jnp.where(side == 0, jnp.concatenate([total, other]), jnp.concatenate([other, total]))


def stencil_tables(courant_x, courant_y, growth, two):
    block = jnp.stack([courant_x, courant_y, growth])
    last, begin = block[:, :, -HALO:], block[:, :, :HALO]
    if two:
        both = shifted(jnp.concatenate([last, begin], axis=2), 0, 1)
        low, high = both[:, :, :HALO], both[:, :, HALO:]
    else:
        low, high = shifted(last, 0, 1), shifted(begin, 0, -1)
    block = jnp.concatenate([low, block, high], axis=2)
    low = shifted(block[:, -HALO:], 1, 0)
    high = shifted(block[:, :HALO], -1, 0)
    block = jnp.concatenate([low, block, high], axis=1)
    cx, cy, gr = block[0], block[1], block[2]
    table = jnp.stack([0.2 + gr, 0.2 - cx, 0.2 + cx, 0.2 - cy, 0.2 + cy])
    times = LANES // EDGE
    return (
        table[:, :, HALO:-HALO],
        jnp.tile(table[:, :, :EDGE], (1, 1, times)),
        jnp.tile(table[:, :, -EDGE:], (1, 1, times)),
    )


def per_device(tangent, courant_x, courant_y, growth):
    fields, rows, cols = tangent.shape
    nx, ny = lax.axis_size("gx"), lax.axis_size("gy")
    two = ny == 2
    tables = stencil_tables(courant_x, courant_y, growth, two)
    own = arrange(tangent)
    low = shifted(own[-HALO:], 1, 0)
    high = shifted(own[:HALO], -1, 0)
    edge = own[:, fields:]

    def sideways(block, down):
        west = shifted(block, down, 1)
        return west, west if two else shifted(block, down, -1)

    west, east = sideways(edge, 0)
    low_west, low_east = sideways(edge[-HALO:], 1)
    high_west, high_east = sideways(edge[:HALO], -1)
    halos = (low, high, west, east, low_west, low_east, high_west, high_east)
    evolved, payload = evolve(own, halos, tables)
    total = float(rows * nx * cols * ny)
    factor, inverse, exponents = factorize(summed(payload), total)
    return project(inverse, evolved, rows), factor, exponents.reshape(fields)


def solution(mesh):
    placed = (P(None, "gx", "gy"), P("gx", "gy"), P("gx", "gy"), P("gx", "gy"))
    return jax.shard_map(
        per_device,
        mesh=mesh,
        in_specs=placed,
        out_specs=(P(None, "gx", "gy"), P(), P()),
        check_vma=False,
    )
```

```python
import functools

import jax
import jax.numpy as jnp
from jax import lax
from jax.experimental import pallas as pl
from jax.experimental.pallas import tpu as pltpu
from jax.sharding import PartitionSpec as P

F32 = jnp.float32
BF16 = jnp.bfloat16
SUBSTEPS = 4
LANES = 128
HALO = SUBSTEPS
GROUP = 8
EDGE = 2 * HALO
PACKED = 16


def spread(row):
    return jnp.broadcast_to(row, (8, 128))

def factor_block(v):
    sub = lax.broadcasted_iota(jnp.int32, (8, 128), 0)
    n = 8
    for p in range(16):
        c0 = p * n
        diag = v[c0:c0 + n, 0:128]
        column = [jnp.broadcast_to(diag[:, c0 + j:c0 + j + 1], (n, 128)) for j in range(n)]
        d = {(i, j): spread(column[j][i:i + 1]) for j in range(n) for i in range(j + 1)}
        inv, r, x = {}, {}, {}
        for j in range(n):
            inv[j] = lax.rsqrt(d[j, j])
            for k in range(j + 1, n):
                r[j, k] = d[j, k] * inv[j]
            for i in range(j + 1, n):
                for k in range(i, n):
                    d[i, k] = d[i, k] - r[j, i] * r[j, k]
        for j in range(n):
            x[j, j] = inv[j]
            for i in range(j + 1, n):
                acc = r[j, i] * x[j, j]
                for k in range(j + 1, i):
                    acc = acc + r[k, i] * x[k, j]
                x[i, j] = -(inv[i] * acc)
        dinv = {}
        for a in range(n):
            for b in range(a, n):
                acc = x[b, a] * x[b, b]
                for m in range(b + 1, n):
                    acc = acc + x[m, a] * x[m, b]
                dinv[a, b] = dinv[b, a] = acc
        ys = []
        for t in range(3):
            cols = slice(128 * t, 128 * t + 128)
            rows = [spread(v[c0 + k:c0 + k + 1, cols]) for k in range(n)]
            ys.append([sum(dinv[a, k] * rows[k] for k in range(n)) for a in range(n)])
            out = x[0, 0] * rows[0]
            for i in range(1, n):
                out = jnp.where(sub == i, sum(x[i, k] * rows[k] for k in range(i + 1)), out)
            v[c0:c0 + n, cols] = out
        for g in range(p + 1, 16):
            ag = v[n * g:n * g + n, 0:128]
            ab = [jnp.broadcast_to(ag[:, c0 + j:c0 + j + 1], (n, 128)) for j in range(n)]
            for t in range(3):
                cols = slice(128 * t, 128 * t + 128)
                acc = v[n * g:n * g + n, cols]
                for j in range(n):
                    acc = acc - ab[j] * ys[t][j]
                v[n * g:n * g + n, cols] = acc

def dot_t(a, b):
    return lax.dot_general(a, b, (((0,), (0,)), ((), ())), precision=lax.Precision.HIGHEST, preferred_element_type=F32)

def factor_kernel(total, pay, factor, inverse, exponents, v):
    h = 128
    ri = lax.broadcasted_iota(jnp.int32, (h, h), 0)
    ci = lax.broadcasted_iota(jnp.int32, (h, h), 1)
    eye = jnp.where(ri == ci, 1.0, 0.0).astype(F32)
    fold = pay[0:h, :] / total
    turned = fold.T
    diag0 = jnp.broadcast_to(pay[2 * h:2 * h + 1, :], (h, h)) / total
    v[:, 0:h] = jnp.where(ri == ci, diag0, jnp.where(ri < ci, turned, fold))
    v[:, h:2 * h] = pay[h:2 * h, :] / total
    v[:, 2 * h:3 * h] = eye
    rest = jnp.where(ri <= ci, fold, turned)
    factor_block(v)
    r00 = jnp.where(ri <= ci, v[:, 0:h], 0.0)
    r01 = v[:, h:2 * h]
    l00 = jnp.where(ri >= ci, v[:, 2 * h:3 * h], 0.0)
    factor[0:h, 0:h] = r00
    factor[0:h, h:2 * h] = r01
    inverse[0:h, 0:h] = l00.astype(jnp.bfloat16)
    inverse[0:h, h:2 * h] = jnp.zeros((h, h), jnp.bfloat16)
    exponents[:, 0:h] = jnp.log(jnp.sum(r00 * eye, axis=0, keepdims=True))
    v[:, 0:h] = rest - dot_t(r01, r01)
    v[:, h:2 * h] = -dot_t(r01, l00)
    v[:, 2 * h:3 * h] = eye
    factor_block(v)
    r11 = jnp.where(ri <= ci, v[:, 0:h], 0.0)
    factor[h:2 * h, 0:h] = jnp.zeros((h, h), F32)
    factor[h:2 * h, h:2 * h] = r11
    inverse[h:2 * h, 0:h] = v[:, h:2 * h].astype(jnp.bfloat16)
    inverse[h:2 * h, h:2 * h] = jnp.where(ri >= ci, v[:, 2 * h:3 * h], 0.0).astype(jnp.bfloat16)
    exponents[:, h:2 * h] = jnp.log(jnp.sum(r11 * eye, axis=0, keepdims=True))

def factorize(pay, total):
    return pl.pallas_call(
        functools.partial(factor_kernel, total),
        out_shape=(jax.ShapeDtypeStruct((256,256),F32), jax.ShapeDtypeStruct((256,256),jnp.bfloat16), jax.ShapeDtypeStruct((1,256),F32)),
        scratch_shapes=[pltpu.VMEM((128,384),F32)],
        compiler_params=pltpu.CompilerParams(vmem_limit_bytes=16<<20),
    )(pay)

def turn_kernel(tangent, turned, wide):
    fields, rows, lanes = tangent.shape
    pitch = rows + 1

    def widen(f, carry):
        wide[pl.ds(f * pitch, rows), :] = tangent[f].astype(F32)
        return carry

    lax.fori_loop(0, fields, widen, 0, unroll=8)

    def turn(r, carry):
        turned[r] = wide[pl.ds(r, fields, stride=pitch), :].T.astype(BF16)
        return carry

    lax.fori_loop(0, rows, turn, 0, unroll=2)


def turn(tangent):
    fields, rows, lanes = tangent.shape
    return pl.pallas_call(
        turn_kernel,
        out_shape=jax.ShapeDtypeStruct((rows, lanes, fields), BF16),
        scratch_shapes=[pltpu.VMEM((fields * (rows + 1), lanes), F32)],
        compiler_params=pltpu.CompilerParams(vmem_limit_bytes=16 << 20),
    )(tangent)


def evolve_kernel(own, low, high, sides, table, evolved, payload, first, second, coef, gram, held):
    rows, lanes, fields = own.shape
    width = lanes + 2 * HALO
    halves = fields // LANES
    start_of = lambda r: GROUP + r * width

    def spread(q, carry):
        for m in range(3):
            line = jnp.broadcast_to(table[m, pl.ds(q, 1)], (LANES, LANES))
            coef[m, pl.ds(pl.multiple_of(q * LANES, LANES), LANES), :] = line.T
        return carry

    lax.fori_loop(0, table.shape[1], spread, 0, unroll=2)

    def fill(row, block):
        for h in range(halves):
            first[h, pl.ds(start_of(row) + HALO, lanes), :] = block[:, LANES * h:LANES * (h + 1)].astype(F32)

    for i in range(HALO):
        fill(i, low[i])
        fill(HALO + rows + i, high[i])

    def fill_own(r, carry):
        fill(HALO + r, own[r])
        return carry

    lax.fori_loop(0, rows, fill_own, 0)

    def fill_sides(r, carry):
        pair = sides[r].astype(F32)
        for h in range(halves):
            first[h, pl.ds(start_of(r), HALO), :] = pair[:HALO, LANES * h:LANES * (h + 1)]
            first[h, pl.ds(start_of(r) + HALO + lanes, HALO), :] = pair[HALO:, LANES * h:LANES * (h + 1)]
        return carry

    lax.fori_loop(0, rows + 2 * HALO, fill_sides, 0)

    def weights(at):
        cx, cy, gr = [coef[m, pl.ds(at, GROUP), :] for m in range(3)]
        return 0.2 + gr, 0.2 - cx, 0.2 + cx, 0.2 - cy, 0.2 + cy

    def combine(f, c, n, s, e, w):
        return f[0] * c + (f[1] * n + f[2] * s) + (f[3] * e + f[4] * w)

    def pair_of(source, at, f):
        for h in range(halves):
            value = [source[h, pl.ds(at + width * i, GROUP), :] for i in range(-1, 3)]
            east = [source[h, pl.ds(at + width * i + 1, GROUP), :] for i in range(2)]
            west = [source[h, pl.ds(at + width * i - 1, GROUP), :] for i in range(2)]
            yield [combine(f[i], value[i + 1], value[i + 2], value[i], east[i], west[i]) for i in range(2)]

    def substep(source, target, step):
        def pair(p, carry):
            r = step + 2 * p
            for t in range(width // GROUP):
                at = pl.multiple_of(start_of(r) + GROUP * t, GROUP)
                f = [weights(at - GROUP + width * i) for i in range(2)]
                for h, out in enumerate(pair_of(source, at, f)):
                    for i in range(2):
                        target[h, pl.ds(at + width * i, GROUP), :] = out[i]
            return carry

        lax.fori_loop(0, (rows + 2 * (HALO - step)) // 2, pair, 0)

    buffers = [first, second]
    for step in range(1, SUBSTEPS):
        substep(buffers[(step - 1) % 2], buffers[step % 2], step)
    source = buffers[(SUBSTEPS - 1) % 2]
    gram[...] = jnp.zeros_like(gram)
    chunk = 8

    def last_chunk(q, carry):
        def pair(p, inner):
            r = q * chunk + 2 * p
            for t in range(0, lanes // GROUP, 2):
                parts = []
                for u in range(2):
                    at = start_of(HALO + r) + HALO + GROUP * (t + u)
                    f = [weights(at - GROUP + width * i) for i in range(2)]
                    parts.append(list(pair_of(source, at, f)))
                for i in range(2):
                    for h in range(halves):
                        both = jnp.concatenate([parts[0][h][i], parts[1][h][i]], axis=0).astype(BF16)
                        evolved[r + i, GROUP * t:GROUP * (t + 2), LANES * h:LANES * (h + 1)] = both
            return inner

        lax.fori_loop(0, chunk // 2, pair, 0)
        part = evolved[pl.ds(q * chunk, chunk)].reshape(chunk * lanes, fields)
        gram[...] += lax.dot_general(part, part, (((0,), (0,)), ((), ())), preferred_element_type=F32)
        return carry

    lax.fori_loop(0, rows // chunk, last_chunk, 0)
    h = fields // 2
    ri = lax.broadcasted_iota(jnp.int32, (h, h), 0)
    ci = lax.broadcasted_iota(jnp.int32, (h, h), 1)
    corner = gram[0:h, 0:h]
    payload[0:h] = jnp.where(ri <= ci, gram[h:2 * h, h:2 * h], corner)
    payload[h:2 * h] = gram[0:h, h:2 * h]
    diagonal = jnp.sum(jnp.where(ri == ci, corner, 0.0), axis=0, keepdims=True)
    payload[2 * h:] = jnp.broadcast_to(diagonal, (PACKED, h))


def evolve(own, low, high, sides, table):
    rows, lanes, fields = own.shape
    width = lanes + 2 * HALO
    state = (fields // LANES, (rows + 2 * HALO) * width + 2 * GROUP, LANES)
    return pl.pallas_call(
        evolve_kernel,
        out_shape=(
            jax.ShapeDtypeStruct((rows, lanes, fields), BF16),
            jax.ShapeDtypeStruct((fields + PACKED, fields // 2), F32),
        ),
        scratch_shapes=[
            pltpu.VMEM(state, F32),
            pltpu.VMEM(state, F32),
            pltpu.VMEM((3, table.shape[1] * LANES, LANES), F32),
            pltpu.VMEM((fields, fields), F32),
            pltpu.VMEM((GROUP, LANES), F32),
        ],
        compiler_params=pltpu.CompilerParams(vmem_limit_bytes=42 << 20),
    )(own, low, high, sides, table)


def project_kernel(inverse, evolved, basis, wide):
    fields, rows, lanes = basis.shape
    pitch = rows + 1
    for r in range(0, rows, 2):
        cells = evolved[r:r + 2].reshape(2 * lanes, fields)
        part = lax.dot_general(inverse[...], cells, (((1,), (1,)), ((), ())), preferred_element_type=F32)
        for i in range(2):
            wide[pl.ds(r + i, fields, stride=pitch), :] = part[:, i * lanes:(i + 1) * lanes]

    def store(f, carry):
        basis[f] = wide[pl.ds(f * pitch, rows), :].astype(BF16)
        return carry

    lax.fori_loop(0, fields, store, 0, unroll=8)


def project(inverse, evolved):
    rows, lanes, fields = evolved.shape
    step = 16
    return pl.pallas_call(
        project_kernel,
        grid=(rows // step,),
        in_specs=[
            pl.BlockSpec((fields, fields), lambda i: (0, 0)),
            pl.BlockSpec((step, lanes, fields), lambda i: (i, 0, 0)),
        ],
        out_specs=pl.BlockSpec((fields, step, lanes), lambda i: (0, i, 0)),
        out_shape=jax.ShapeDtypeStruct((fields, rows, lanes), BF16),
        scratch_shapes=[pltpu.VMEM(((step + 1) * fields, lanes), F32)],
        compiler_params=pltpu.CompilerParams(vmem_limit_bytes=32 << 20),
    )(inverse, evolved)


def shifted(block, down, right):
    nx, ny = lax.axis_size("gx"), lax.axis_size("gy")
    pairs = []
    for x in range(nx):
        for y in range(ny):
            pairs.append((x * ny + y, (x + down) % nx * ny + (y + right) % ny))
    return lax.ppermute(block, ("gx", "gy"), pairs)


def swapped(block, axis, bit):
    return lax.ppermute(block, axis, [(i, i ^ bit) for i in range(lax.axis_size(axis))])


def summed(payload):
    nx, ny = lax.axis_size("gx"), lax.axis_size("gy")
    if nx & (nx - 1) or ny & (ny - 1) or nx < 2:
        return lax.psum(payload, ("gx", "gy"))
    half = payload.shape[0] // 2
    side = lax.axis_index("gx") % 2
    kept = lax.dynamic_slice_in_dim(payload, side * half, half, 0)
    given = lax.dynamic_slice_in_dim(payload, (1 - side) * half, half, 0)
    total = kept + swapped(given, "gx", 1)
    for axis, bits in (("gy", range(ny.bit_length() - 1)), ("gx", range(1, nx.bit_length() - 1))):
        for bit in bits:
            total = total + swapped(total, axis, 1 << bit)
    other = swapped(total, "gx", 1)
    return jnp.where(side == 0, jnp.concatenate([total, other]), jnp.concatenate([other, total]))


def pieces(block):
    out = []
    for _ in range(3):
        part = lax.reduce_precision(block, 8, 7)
        out.append(part.astype(BF16))
        block = block - part
    return jnp.concatenate(out)


def joined(parts):
    count = parts.shape[0] // 3
    wide = parts.astype(F32)
    return wide[:count] + wide[count:2 * count] + wide[2 * count:]


def loaded(state, parts):
    fields = state.shape[-1]
    flat = parts.reshape(-1)
    flat = jnp.pad(flat, (0, -flat.size % (PACKED * fields)))
    return jnp.concatenate([state.reshape(-1, fields), flat.reshape(-1, fields)])


def unloaded(matrix, rows, cols):
    cells = rows * cols
    parts = matrix[cells:].reshape(-1)[:9 * cells].reshape(9, rows, cols)
    return matrix[:cells].reshape(rows, cols, -1), joined(parts)


def per_device(tangent, courant_x, courant_y, growth):
    fields, rows, cols = tangent.shape
    nx, ny = lax.axis_size("gx"), lax.axis_size("gy")
    block = jnp.stack([courant_x, courant_y, growth])
    parts = pieces(block)
    own = turn(tangent)

    def edges(x, axis):
        size = x.shape[axis]
        return lax.slice_in_dim(x, size - HALO, size, axis=axis), lax.slice_in_dim(x, 0, HALO, axis=axis)

    def sideways(state, part, down):
        state_last, state_begin = edges(state, 1)
        part_last, part_begin = edges(part, 2)
        count = state.shape[0]
        if ny == 2:
            both = loaded(jnp.concatenate([state_last, state_begin], axis=1), jnp.concatenate([part_last, part_begin], axis=2))
            return unloaded(shifted(both, down, 1), count, 2 * HALO)
        west = unloaded(shifted(loaded(state_last, part_last), down, 1), count, HALO)
        east = unloaded(shifted(loaded(state_begin, part_begin), down, -1), count, HALO)
        return jnp.concatenate([west[0], east[0]], axis=1), jnp.concatenate([west[1], east[1]], axis=2)

    side = sideways(own, parts, 0)
    state_last, state_begin = edges(own, 0)
    part_last, part_begin = edges(parts, 1)
    low = unloaded(shifted(loaded(state_last, part_last), 1, 0), HALO, cols)
    high = unloaded(shifted(loaded(state_begin, part_begin), -1, 0), HALO, cols)
    low_side = sideways(state_last, part_last, 1)
    high_side = sideways(state_begin, part_begin, -1)
    sides = jnp.concatenate([low_side[0], side[0], high_side[0]])
    middle = jnp.concatenate([low[1], block, high[1]], axis=1)
    around = jnp.concatenate([low_side[1], side[1], high_side[1]], axis=1)
    table = jnp.concatenate([around[:, :, :HALO], middle, around[:, :, HALO:]], axis=2).reshape(3, -1)
    table = jnp.pad(table, ((0, 0), (0, -table.shape[1] % LANES))).reshape(3, -1, LANES)
    evolved, payload = evolve(own, low[0], high[0], sides, table)
    total = float(rows * nx * cols * ny)
    factor, inverse, exponents = factorize(summed(payload), total)
    return project(inverse, evolved), factor, exponents.reshape(fields)


def solution(mesh):
    placed = (P(None, "gx", "gy"), P("gx", "gy"), P("gx", "gy"), P("gx", "gy"))
    return jax.shard_map(
        per_device,
        mesh=mesh,
        in_specs=placed,
        out_specs=(P(None, "gx", "gy"), P(), P()),
        check_vma=False,
    )
```

```python
import functools

import jax
import jax.numpy as jnp
from jax import lax
from jax.experimental import pallas as pl
from jax.experimental.pallas import tpu as pltpu
from jax.sharding import PartitionSpec as P

F32 = jnp.float32
BF16 = jnp.bfloat16
SUBSTEPS = 4
LANES = 128
HALO = SUBSTEPS
GROUP = 8
EDGE = 2 * HALO
PACKED = 16


def spread(row):
    return jnp.broadcast_to(row, (8, 128))

def factor_block(v):
    sub = lax.broadcasted_iota(jnp.int32, (8, 128), 0)
    n = 8
    for p in range(16):
        c0 = p * n
        diag = v[c0:c0 + n, 0:128]
        column = [jnp.broadcast_to(diag[:, c0 + j:c0 + j + 1], (n, 128)) for j in range(n)]
        d = {(i, j): spread(column[j][i:i + 1]) for j in range(n) for i in range(j + 1)}
        inv, r, x = {}, {}, {}
        for j in range(n):
            inv[j] = lax.rsqrt(d[j, j])
            for k in range(j + 1, n):
                r[j, k] = d[j, k] * inv[j]
            for i in range(j + 1, n):
                for k in range(i, n):
                    d[i, k] = d[i, k] - r[j, i] * r[j, k]
        for j in range(n):
            x[j, j] = inv[j]
            for i in range(j + 1, n):
                acc = r[j, i] * x[j, j]
                for k in range(j + 1, i):
                    acc = acc + r[k, i] * x[k, j]
                x[i, j] = -(inv[i] * acc)
        dinv = {}
        for a in range(n):
            for b in range(a, n):
                acc = x[b, a] * x[b, b]
                for m in range(b + 1, n):
                    acc = acc + x[m, a] * x[m, b]
                dinv[a, b] = dinv[b, a] = acc
        ys = []
        for t in range(3):
            cols = slice(128 * t, 128 * t + 128)
            rows = [spread(v[c0 + k:c0 + k + 1, cols]) for k in range(n)]
            ys.append([sum(dinv[a, k] * rows[k] for k in range(n)) for a in range(n)])
            out = x[0, 0] * rows[0]
            for i in range(1, n):
                out = jnp.where(sub == i, sum(x[i, k] * rows[k] for k in range(i + 1)), out)
            v[c0:c0 + n, cols] = out
        for g in range(p + 1, 16):
            ag = v[n * g:n * g + n, 0:128]
            ab = [jnp.broadcast_to(ag[:, c0 + j:c0 + j + 1], (n, 128)) for j in range(n)]
            for t in range(3):
                cols = slice(128 * t, 128 * t + 128)
                acc = v[n * g:n * g + n, cols]
                for j in range(n):
                    acc = acc - ab[j] * ys[t][j]
                v[n * g:n * g + n, cols] = acc

def dot_t(a, b):
    return lax.dot_general(a, b, (((0,), (0,)), ((), ())), precision=lax.Precision.HIGHEST, preferred_element_type=F32)

def factor_kernel(total, pay, factor, inverse, exponents, v):
    h = 128
    ri = lax.broadcasted_iota(jnp.int32, (h, h), 0)
    ci = lax.broadcasted_iota(jnp.int32, (h, h), 1)
    eye = jnp.where(ri == ci, 1.0, 0.0).astype(F32)
    fold = pay[0:h, :] / total
    turned = fold.T
    diag0 = jnp.broadcast_to(pay[2 * h:2 * h + 1, :], (h, h)) / total
    v[:, 0:h] = jnp.where(ri == ci, diag0, jnp.where(ri < ci, turned, fold))
    v[:, h:2 * h] = pay[h:2 * h, :] / total
    v[:, 2 * h:3 * h] = eye
    rest = jnp.where(ri <= ci, fold, turned)
    factor_block(v)
    r00 = jnp.where(ri <= ci, v[:, 0:h], 0.0)
    r01 = v[:, h:2 * h]
    l00 = jnp.where(ri >= ci, v[:, 2 * h:3 * h], 0.0)
    factor[0:h, 0:h] = r00
    factor[0:h, h:2 * h] = r01
    inverse[0:h, 0:h] = l00.astype(jnp.bfloat16)
    inverse[0:h, h:2 * h] = jnp.zeros((h, h), jnp.bfloat16)
    exponents[:, 0:h] = jnp.log(jnp.sum(r00 * eye, axis=0, keepdims=True))
    v[:, 0:h] = rest - dot_t(r01, r01)
    v[:, h:2 * h] = -dot_t(r01, l00)
    v[:, 2 * h:3 * h] = eye
    factor_block(v)
    r11 = jnp.where(ri <= ci, v[:, 0:h], 0.0)
    factor[h:2 * h, 0:h] = jnp.zeros((h, h), F32)
    factor[h:2 * h, h:2 * h] = r11
    inverse[h:2 * h, 0:h] = v[:, h:2 * h].astype(jnp.bfloat16)
    inverse[h:2 * h, h:2 * h] = jnp.where(ri >= ci, v[:, 2 * h:3 * h], 0.0).astype(jnp.bfloat16)
    exponents[:, h:2 * h] = jnp.log(jnp.sum(r11 * eye, axis=0, keepdims=True))


def turn_kernel(source, target, tangent, wide, turned, read, write):
    fields, rows, lanes = tangent.shape
    pitch = rows + 1
    chunks = read.shape[0]
    each, lines = fields // chunks, rows // chunks

    def loading(q):
        return pltpu.make_async_copy(source.at[pl.ds(q * each, each)], tangent.at[pl.ds(q * each, each)], read.at[q])

    def storing(q):
        return pltpu.make_async_copy(turned.at[pl.ds(q * lines, lines)], target.at[pl.ds(q * lines, lines)], write.at[q])

    for q in range(chunks):
        loading(q).start()

    def widen(f, carry):
        wide[pl.ds(f * pitch, rows), :] = tangent[f].astype(F32)
        return carry

    for q in range(chunks):
        loading(q).wait()
        lax.fori_loop(q * each, (q + 1) * each, widen, 0, unroll=8)

    def turn_row(r, carry):
        turned[r] = wide[pl.ds(r, fields, stride=pitch), :].T.astype(BF16)
        return carry

    for q in range(chunks):
        lax.fori_loop(q * lines, (q + 1) * lines, turn_row, 0, unroll=2)
        storing(q).start()
    for q in range(chunks):
        storing(q).wait()


def turn(tangent):
    fields, rows, lanes = tangent.shape
    chunks = 8
    return pl.pallas_call(
        turn_kernel,
        in_specs=[pl.BlockSpec(memory_space=pltpu.HBM)],
        out_specs=pl.BlockSpec(memory_space=pltpu.HBM),
        out_shape=pltpu.HBM((rows, lanes, fields), BF16),
        scratch_shapes=[
            pltpu.VMEM((fields, rows, lanes), BF16),
            pltpu.VMEM((fields * (rows + 1), lanes), F32),
            pltpu.VMEM((rows, lanes, fields), BF16),
            pltpu.SemaphoreType.DMA((chunks,)),
            pltpu.SemaphoreType.DMA((chunks,)),
        ],
        compiler_params=pltpu.CompilerParams(vmem_limit_bytes=24 << 20),
    )(pltpu.with_memory_space_constraint(tangent, pltpu.HBM))


def evolve_kernel(source_block, low, high, sides, table, target_block, payload, first, second, coef, gram, own, read, write):
    rows, lanes, fields = own.shape
    evolved = own
    chunks = read.shape[0]
    lines = rows // chunks

    def loading(q):
        return pltpu.make_async_copy(source_block.at[pl.ds(q * lines, lines)], own.at[pl.ds(q * lines, lines)], read.at[q])

    def storing(q):
        return pltpu.make_async_copy(
            evolved.at[pl.ds(q * lines, lines)], target_block.at[pl.ds(q * lines, lines)], write.at[q])

    for q in range(chunks):
        loading(q).start()
    width = lanes + 2 * HALO
    halves = fields // LANES
    start_of = lambda r: GROUP + r * width

    def spread(q, carry):
        for m in range(3):
            line = jnp.broadcast_to(table[m, pl.ds(q, 1)], (LANES, LANES))
            coef[m, pl.ds(pl.multiple_of(q * LANES, LANES), LANES), :] = line.T
        return carry

    lax.fori_loop(0, table.shape[1], spread, 0, unroll=2)

    def fill(row, block):
        for h in range(halves):
            first[h, pl.ds(start_of(row) + HALO, lanes), :] = block[:, LANES * h:LANES * (h + 1)].astype(F32)

    for i in range(HALO):
        fill(i, low[i])
        fill(HALO + rows + i, high[i])

    def fill_own(r, carry):
        fill(HALO + r, own[r])
        return carry

    for q in range(chunks):
        loading(q).wait()
        lax.fori_loop(q * lines, (q + 1) * lines, fill_own, 0)

    def fill_sides(r, carry):
        pair = sides[r].astype(F32)
        for h in range(halves):
            first[h, pl.ds(start_of(r), HALO), :] = pair[:HALO, LANES * h:LANES * (h + 1)]
            first[h, pl.ds(start_of(r) + HALO + lanes, HALO), :] = pair[HALO:, LANES * h:LANES * (h + 1)]
        return carry

    lax.fori_loop(0, rows + 2 * HALO, fill_sides, 0)

    def weights(at):
        cx, cy, gr = [coef[m, pl.ds(at, GROUP), :] for m in range(3)]
        return 0.2 + gr, 0.2 - cx, 0.2 + cx, 0.2 - cy, 0.2 + cy

    def combine(f, c, n, s, e, w):
        return f[0] * c + (f[1] * n + f[2] * s) + (f[3] * e + f[4] * w)

    def pair_of(source, at, f):
        for h in range(halves):
            value = [source[h, pl.ds(at + width * i, GROUP), :] for i in range(-1, 3)]
            east = [source[h, pl.ds(at + width * i + 1, GROUP), :] for i in range(2)]
            west = [source[h, pl.ds(at + width * i - 1, GROUP), :] for i in range(2)]
            yield [combine(f[i], value[i + 1], value[i + 2], value[i], east[i], west[i]) for i in range(2)]

    def substep(source, target, step):
        def pair(p, carry):
            r = step + 2 * p
            for t in range(width // GROUP):
                at = pl.multiple_of(start_of(r) + GROUP * t, GROUP)
                f = [weights(at - GROUP + width * i) for i in range(2)]
                for h, out in enumerate(pair_of(source, at, f)):
                    for i in range(2):
                        target[h, pl.ds(at + width * i, GROUP), :] = out[i]
            return carry

        lax.fori_loop(0, (rows + 2 * (HALO - step)) // 2, pair, 0)

    buffers = [first, second]
    for step in range(1, SUBSTEPS):
        substep(buffers[(step - 1) % 2], buffers[step % 2], step)
    source = buffers[(SUBSTEPS - 1) % 2]
    gram[...] = jnp.zeros_like(gram)
    chunk = lines

    def last_chunk(q, carry):
        def pair(p, inner):
            r = q * chunk + 2 * p
            for t in range(0, lanes // GROUP, 2):
                parts = []
                for u in range(2):
                    at = start_of(HALO + r) + HALO + GROUP * (t + u)
                    f = [weights(at - GROUP + width * i) for i in range(2)]
                    parts.append(list(pair_of(source, at, f)))
                for i in range(2):
                    for h in range(halves):
                        both = jnp.concatenate([parts[0][h][i], parts[1][h][i]], axis=0).astype(BF16)
                        evolved[r + i, GROUP * t:GROUP * (t + 2), LANES * h:LANES * (h + 1)] = both
            return inner

        lax.fori_loop(0, chunk // 2, pair, 0)
        part = evolved[pl.ds(q * chunk, chunk)].reshape(chunk * lanes, fields)
        gram[...] += lax.dot_general(part, part, (((0,), (0,)), ((), ())), preferred_element_type=F32)
        storing(q).start()
        return carry

    lax.fori_loop(0, chunks, last_chunk, 0)
    h = fields // 2
    ri = lax.broadcasted_iota(jnp.int32, (h, h), 0)
    ci = lax.broadcasted_iota(jnp.int32, (h, h), 1)
    corner = gram[0:h, 0:h]
    payload[0:h] = jnp.where(ri <= ci, gram[h:2 * h, h:2 * h], corner)
    payload[h:2 * h] = gram[0:h, h:2 * h]
    diagonal = jnp.sum(jnp.where(ri == ci, corner, 0.0), axis=0, keepdims=True)
    payload[2 * h:] = jnp.broadcast_to(diagonal, (PACKED, h))
    for q in range(chunks):
        storing(q).wait()


def evolve(own, low, high, sides, table):
    rows, lanes, fields = own.shape
    width = lanes + 2 * HALO
    state = (fields // LANES, (rows + 2 * HALO) * width + 2 * GROUP, LANES)
    chunks = 8
    hbm, vmem = pl.BlockSpec(memory_space=pltpu.HBM), pl.BlockSpec(memory_space=pltpu.VMEM)
    return pl.pallas_call(
        evolve_kernel,
        in_specs=[hbm, vmem, vmem, vmem, vmem],
        out_specs=(hbm, vmem),
        out_shape=(
            pltpu.HBM((rows, lanes, fields), BF16),
            jax.ShapeDtypeStruct((fields + PACKED, fields // 2), F32),
        ),
        scratch_shapes=[
            pltpu.VMEM(state, F32),
            pltpu.VMEM(state, F32),
            pltpu.VMEM((3, table.shape[1] * LANES, LANES), F32),
            pltpu.VMEM((fields, fields), F32),
            pltpu.VMEM((rows, lanes, fields), BF16),
            pltpu.SemaphoreType.DMA((chunks,)),
            pltpu.SemaphoreType.DMA((chunks,)),
        ],
        compiler_params=pltpu.CompilerParams(vmem_limit_bytes=42 << 20),
    )(pltpu.with_memory_space_constraint(own, pltpu.HBM), low, high, sides, table)


def finish_kernel(total, pay, source, factor, exponents, basis, v, inverse, evolved, wide, out, read, write):
    rows, lanes, fields = evolved.shape
    chunks, step = out.shape[0], out.shape[2]
    pitch = step + 1

    def loading(q):
        return pltpu.make_async_copy(source.at[pl.ds(q * step, step)], evolved.at[pl.ds(q * step, step)], read.at[q])

    def storing(q):
        return pltpu.make_async_copy(out.at[q], basis.at[:, pl.ds(q * step, step)], write.at[q])

    for q in range(chunks):
        loading(q).start()
    factor_kernel(total, pay, factor, inverse, exponents, v)
    for q in range(chunks):
        loading(q).wait()
        for r in range(0, step, 2):
            cells = evolved[q * step + r:q * step + r + 2].reshape(2 * lanes, fields)
            part = lax.dot_general(inverse[...], cells, (((1,), (1,)), ((), ())), preferred_element_type=F32)
            for i in range(2):
                wide[pl.ds(r + i, fields, stride=pitch), :] = part[:, i * lanes:(i + 1) * lanes]

        def narrow(f, carry):
            out[q, f] = wide[pl.ds(f * pitch, step), :].astype(BF16)
            return carry

        lax.fori_loop(0, fields, narrow, 0, unroll=8)
        storing(q).start()
    for q in range(chunks):
        storing(q).wait()


def finish(pay, evolved, total):
    rows, lanes, fields = evolved.shape
    step = 16
    chunks = rows // step
    hbm, vmem = pl.BlockSpec(memory_space=pltpu.HBM), pl.BlockSpec(memory_space=pltpu.VMEM)
    return pl.pallas_call(
        functools.partial(finish_kernel, total),
        in_specs=[vmem, hbm],
        out_specs=(vmem, vmem, hbm),
        out_shape=(
            jax.ShapeDtypeStruct((fields, fields), F32),
            jax.ShapeDtypeStruct((1, fields), F32),
            jax.ShapeDtypeStruct((fields, rows, lanes), BF16),
        ),
        scratch_shapes=[
            pltpu.VMEM((LANES, 3 * LANES), F32),
            pltpu.VMEM((fields, fields), BF16),
            pltpu.VMEM((rows, lanes, fields), BF16),
            pltpu.VMEM(((step + 1) * fields, lanes), F32),
            pltpu.VMEM((chunks, fields, step, lanes), BF16),
            pltpu.SemaphoreType.DMA((chunks,)),
            pltpu.SemaphoreType.DMA((chunks,)),
        ],
        compiler_params=pltpu.CompilerParams(vmem_limit_bytes=24 << 20),
    )(pay, pltpu.with_memory_space_constraint(evolved, pltpu.HBM))


def shifted(block, down, right):
    nx, ny = lax.axis_size("gx"), lax.axis_size("gy")
    pairs = []
    for x in range(nx):
        for y in range(ny):
            pairs.append((x * ny + y, (x + down) % nx * ny + (y + right) % ny))
    return lax.ppermute(block, ("gx", "gy"), pairs)


def swapped(block, axis, bit):
    return lax.ppermute(block, axis, [(i, i ^ bit) for i in range(lax.axis_size(axis))])


def summed(payload):
    nx, ny = lax.axis_size("gx"), lax.axis_size("gy")
    if nx & (nx - 1) or ny & (ny - 1) or nx < 2:
        return lax.psum(payload, ("gx", "gy"))
    half = payload.shape[0] // 2
    side = lax.axis_index("gx") % 2
    kept = lax.dynamic_slice_in_dim(payload, side * half, half, 0)
    given = lax.dynamic_slice_in_dim(payload, (1 - side) * half, half, 0)
    total = kept + swapped(given, "gx", 1)
    for axis, bits in (("gy", range(ny.bit_length() - 1)), ("gx", range(1, nx.bit_length() - 1))):
        for bit in bits:
            total = total + swapped(total, axis, 1 << bit)
    other = swapped(total, "gx", 1)
    return jnp.where(side == 0, jnp.concatenate([total, other]), jnp.concatenate([other, total]))


def pieces(block):
    out = []
    for _ in range(3):
        part = lax.reduce_precision(block, 8, 7)
        out.append(part.astype(BF16))
        block = block - part
    return jnp.concatenate(out)


def joined(parts):
    count = parts.shape[0] // 3
    wide = parts.astype(F32)
    return wide[:count] + wide[count:2 * count] + wide[2 * count:]


def loaded(state, parts):
    fields = state.shape[-1]
    flat = parts.reshape(-1)
    flat = jnp.pad(flat, (0, -flat.size % (PACKED * fields)))
    return jnp.concatenate([state.reshape(-1, fields), flat.reshape(-1, fields)])


def unloaded(matrix, rows, cols):
    cells = rows * cols
    parts = matrix[cells:].reshape(-1)[:9 * cells].reshape(9, rows, cols)
    return matrix[:cells].reshape(rows, cols, -1), parts


def per_device(tangent, courant_x, courant_y, growth):
    fields, rows, cols = tangent.shape
    nx, ny = lax.axis_size("gx"), lax.axis_size("gy")
    block = jnp.stack([courant_x, courant_y, growth])
    parts = pieces(block)
    own = turn(tangent)

    def edges(x, axis):
        size = x.shape[axis]
        return lax.slice_in_dim(x, size - HALO, size, axis=axis), lax.slice_in_dim(x, 0, HALO, axis=axis)

    state_last, state_begin = edges(own, 1)
    part_last, part_begin = edges(parts, 2)
    if ny == 2:
        both = loaded(jnp.concatenate([state_last, state_begin], axis=1), jnp.concatenate([part_last, part_begin], axis=2))
        side, side_part = unloaded(shifted(both, 0, 1), rows, 2 * HALO)
    else:
        west, west_part = unloaded(shifted(loaded(state_last, part_last), 0, 1), rows, HALO)
        east, east_part = unloaded(shifted(loaded(state_begin, part_begin), 0, -1), rows, HALO)
        side, side_part = jnp.concatenate([west, east], axis=1), jnp.concatenate([west_part, east_part], axis=2)

    def ends(state, part, count):
        state_last, state_begin = edges(state, 0)
        part_last, part_begin = edges(part, 1)
        return (unloaded(shifted(loaded(state_last, part_last), 1, 0), HALO, count),
                unloaded(shifted(loaded(state_begin, part_begin), -1, 0), HALO, count))

    low, high = ends(own, parts, cols)
    low_side, high_side = ends(side, side_part, 2 * HALO)
    sides = jnp.concatenate([low_side[0], side, high_side[0]])
    middle = jnp.concatenate([joined(low[1]), block, joined(high[1])], axis=1)
    around = joined(jnp.concatenate([low_side[1], side_part, high_side[1]], axis=1))
    table = jnp.concatenate([around[:, :, :HALO], middle, around[:, :, HALO:]], axis=2).reshape(3, -1)
    table = jnp.pad(table, ((0, 0), (0, -table.shape[1] % LANES))).reshape(3, -1, LANES)
    evolved, payload = evolve(own, low[0], high[0], sides, table)
    total = float(rows * nx * cols * ny)
    factor, exponents, basis = finish(summed(payload), evolved, total)
    return basis, factor, exponents.reshape(fields)


def solution(mesh):
    placed = (P(None, "gx", "gy"), P("gx", "gy"), P("gx", "gy"), P("gx", "gy"))
    return jax.shard_map(
        per_device,
        mesh=mesh,
        in_specs=placed,
        out_specs=(P(None, "gx", "gy"), P(), P()),
        check_vma=False,
    )
```

```python
import functools

import jax
import jax.numpy as jnp
from jax import lax
from jax.experimental import pallas as pl
from jax.experimental.pallas import tpu as pltpu
from jax.sharding import PartitionSpec as P

F32 = jnp.float32
BF16 = jnp.bfloat16
SUBSTEPS = 4
LANES = 128
HALO = SUBSTEPS
GROUP = 8
EDGE = 2 * HALO
PACKED = 16


def tree(terms):
    while len(terms) > 1:
        terms = [a + b for a, b in zip(terms[::2], terms[1::2])] + terms[len(terms) & ~1:]
    return terms[0]


def spread(ref, *at):
    *block, row = at
    return ref[(*block, pl.ds(row, GROUP, stride=0), slice(None))]


def factor_block(v, held):
    sub = lax.broadcasted_iota(jnp.int32, (8, 128), 0)
    n = 8
    for p in range(16):
        c0 = p * n
        diag = v[0, c0:c0 + n]
        column = [jnp.broadcast_to(diag[:, c0 + j:c0 + j + 1], (n, 128)) for j in range(n)]
        base = p % 2 * n * n
        for j in range(n):
            held[base + n * j:base + n * (j + 1)] = column[j]
        d = {(i, j): spread(held, base + n * j + i) for j in range(n) for i in range(j + 1)}
        inv, r, x = {}, {}, {}
        for j in range(n):
            inv[j] = lax.rsqrt(d[j, j])
            for k in range(j + 1, n):
                r[j, k] = d[j, k] * inv[j]
            for i in range(j + 1, n):
                for k in range(i, n):
                    d[i, k] = d[i, k] - r[j, i] * r[j, k]
        for j in range(n):
            x[j, j] = inv[j]
            for i in range(j + 1, n):
                x[i, j] = -(inv[i] * tree([r[k, i] * x[k, j] for k in range(j, i)]))
        dinv = {}
        for a in range(n):
            for b in range(a, n):
                dinv[a, b] = dinv[b, a] = tree([x[m, a] * x[m, b] for m in range(b, n)])
        ys = []
        for t in range(3):
            rows = [spread(v, t, c0 + k) for k in range(n)]
            ys.append([tree([dinv[a, k] * rows[k] for k in range(n)]) for a in range(n)])
            out = x[0, 0] * rows[0]
            for i in range(1, n):
                out = jnp.where(sub == i, tree([x[i, k] * rows[k] for k in range(i + 1)]), out)
            v[t, c0:c0 + n] = out
        for g in range(p + 1, 16):
            ag = v[0, n * g:n * g + n]
            ab = [jnp.broadcast_to(ag[:, c0 + j:c0 + j + 1], (n, 128)) for j in range(n)]
            for t in range(3):
                v[t, n * g:n * g + n] = v[t, n * g:n * g + n] - tree([ab[j] * ys[t][j] for j in range(n)])

def dot_t(a, b):
    return lax.dot_general(a, b, (((0,), (0,)), ((), ())), precision=lax.Precision.HIGHEST, preferred_element_type=F32)

def factor_kernel(total, pay, factor, inverse, exponents, v, held):
    h = 128
    ri = lax.broadcasted_iota(jnp.int32, (h, h), 0)
    ci = lax.broadcasted_iota(jnp.int32, (h, h), 1)
    eye = jnp.where(ri == ci, 1.0, 0.0).astype(F32)
    fold = pay[0:h, :] / total
    turned = fold.T
    diag0 = jnp.broadcast_to(pay[2 * h:2 * h + 1, :], (h, h)) / total
    v[0] = jnp.where(ri == ci, diag0, jnp.where(ri < ci, turned, fold))
    v[1] = pay[h:2 * h, :] / total
    v[2] = eye
    rest = jnp.where(ri <= ci, fold, turned)
    factor_block(v, held)
    r00 = jnp.where(ri <= ci, v[0], 0.0)
    r01 = v[1]
    l00 = jnp.where(ri >= ci, v[2], 0.0)
    factor[0:h, 0:h] = r00
    factor[0:h, h:2 * h] = r01
    inverse[0:h, 0:h] = l00.astype(jnp.bfloat16)
    inverse[0:h, h:2 * h] = jnp.zeros((h, h), jnp.bfloat16)
    exponents[:, 0:h] = jnp.log(jnp.sum(r00 * eye, axis=0, keepdims=True))
    v[0] = rest - dot_t(r01, r01)
    v[1] = -dot_t(r01, l00)
    v[2] = eye
    factor_block(v, held)
    r11 = jnp.where(ri <= ci, v[0], 0.0)
    factor[h:2 * h, 0:h] = jnp.zeros((h, h), F32)
    factor[h:2 * h, h:2 * h] = r11
    inverse[h:2 * h, 0:h] = v[1].astype(jnp.bfloat16)
    inverse[h:2 * h, h:2 * h] = jnp.where(ri >= ci, v[2], 0.0).astype(jnp.bfloat16)
    exponents[:, h:2 * h] = jnp.log(jnp.sum(r11 * eye, axis=0, keepdims=True))


def turn_kernel(source, low_tail, high_tail, side_tail, target, last, begin, side, tangent, wide, turned, read, write):
    fields, rows, lanes = tangent.shape
    pitch = rows + 1
    chunks = read.shape[0]
    each, lines = fields // chunks, rows // chunks

    def loading(q):
        return pltpu.make_async_copy(source.at[pl.ds(q * each, each)], tangent.at[pl.ds(q * each, each)], read.at[q])

    def storing(q):
        return pltpu.make_async_copy(turned.at[pl.ds(q * lines, lines)], target.at[pl.ds(q * lines, lines)], write.at[q])

    for q in range(chunks):
        loading(q).start()

    def widen(f, carry):
        wide[pl.ds(f * pitch, rows), :] = tangent[f].astype(F32)
        return carry

    for q in range(chunks):
        loading(q).wait()
        lax.fori_loop(q * each, (q + 1) * each, widen, 0, unroll=8)

    def turn_rows(p, carry):
        ends = []
        for i in range(2):
            r = 2 * p + i
            line = wide[pl.ds(r, fields, stride=pitch), :].T
            turned[r] = line.astype(BF16)
            ends += [line[lanes - HALO:], line[:HALO]]
        side[pl.ds(pl.multiple_of(p * 4 * HALO, 4 * HALO), 4 * HALO), :] = jnp.concatenate(ends).astype(BF16)
        return carry

    for q in range(chunks):
        lax.fori_loop(q * lines // 2, (q + 1) * lines // 2, turn_rows, 0)
        storing(q).start()
    count = HALO * lanes
    last[0:count] = turned[rows - HALO:].reshape(count, fields)
    last[count:] = low_tail[...]
    begin[0:count] = turned[:HALO].reshape(count, fields)
    begin[count:] = high_tail[...]
    side[2 * HALO * rows:] = side_tail[...]
    for q in range(chunks):
        storing(q).wait()


def turn(tangent, tails):
    fields, rows, lanes = tangent.shape
    chunks = 8
    hbm, vmem = pl.BlockSpec(memory_space=pltpu.HBM), pl.BlockSpec(memory_space=pltpu.VMEM)
    matrix = [jax.ShapeDtypeStruct((cells + tail.shape[0], fields), BF16)
              for cells, tail in zip((HALO * lanes, HALO * lanes, 2 * HALO * rows), tails)]
    return pl.pallas_call(
        turn_kernel,
        in_specs=[hbm, vmem, vmem, vmem],
        out_specs=(hbm, vmem, vmem, vmem),
        out_shape=(pltpu.HBM((rows, lanes, fields), BF16), *matrix),
        scratch_shapes=[
            pltpu.VMEM((fields, rows, lanes), BF16),
            pltpu.VMEM((fields * (rows + 1), lanes), F32),
            pltpu.VMEM((rows, lanes, fields), BF16),
            pltpu.SemaphoreType.DMA((chunks,)),
            pltpu.SemaphoreType.DMA((chunks,)),
        ],
        compiler_params=pltpu.CompilerParams(vmem_limit_bytes=24 << 20),
    )(pltpu.with_memory_space_constraint(tangent, pltpu.HBM), *tails)


def evolve_kernel(source_block, low, high, sides, table, target_block, payload, first, second, coef, gram, own, read, write):
    rows, lanes, fields = own.shape
    evolved = own
    chunks = read.shape[0]
    lines = rows // chunks

    def loading(q):
        return pltpu.make_async_copy(source_block.at[pl.ds(q * lines, lines)], own.at[pl.ds(q * lines, lines)], read.at[q])

    def storing(q):
        return pltpu.make_async_copy(
            evolved.at[pl.ds(q * lines, lines)], target_block.at[pl.ds(q * lines, lines)], write.at[q])

    for q in range(chunks):
        loading(q).start()
    width = lanes + 2 * HALO
    halves = fields // LANES
    start_of = lambda r: GROUP + r * width

    for m in range(3):
        turned_table = jnp.concatenate([table[m], jnp.zeros((LANES - table.shape[1], LANES), F32)]).T
        for q in range(table.shape[1]):
            coef[m, LANES * q:LANES * (q + 1), :] = jnp.broadcast_to(turned_table[:, q:q + 1], (LANES, LANES))

    def fill(row, block):
        for h in range(halves):
            first[h, pl.ds(start_of(row) + HALO, lanes), :] = block[:, LANES * h:LANES * (h + 1)].astype(F32)

    for i in range(HALO):
        fill(i, low[i])
        fill(HALO + rows + i, high[i])

    def fill_own(r, carry):
        fill(HALO + r, own[r])
        return carry

    for q in range(chunks):
        loading(q).wait()
        lax.fori_loop(q * lines, (q + 1) * lines, fill_own, 0)

    def fill_sides(r, carry):
        pair = sides[r].astype(F32)
        for h in range(halves):
            first[h, pl.ds(start_of(r), HALO), :] = pair[:HALO, LANES * h:LANES * (h + 1)]
            first[h, pl.ds(start_of(r) + HALO + lanes, HALO), :] = pair[HALO:, LANES * h:LANES * (h + 1)]
        return carry

    lax.fori_loop(0, rows + 2 * HALO, fill_sides, 0)

    def weights(at):
        cx, cy, gr = [coef[m, pl.ds(at, GROUP), :] for m in range(3)]
        return 0.2 + gr, 0.2 - cx, 0.2 + cx, 0.2 - cy, 0.2 + cy

    def combine(f, c, n, s, e, w):
        return f[0] * c + (f[1] * n + f[2] * s) + (f[3] * e + f[4] * w)

    def pair_of(source, at, f):
        for h in range(halves):
            value = [source[h, pl.ds(at + width * i, GROUP), :] for i in range(-1, 3)]
            east = [source[h, pl.ds(at + width * i + 1, GROUP), :] for i in range(2)]
            west = [source[h, pl.ds(at + width * i - 1, GROUP), :] for i in range(2)]
            yield [combine(f[i], value[i + 1], value[i + 2], value[i], east[i], west[i]) for i in range(2)]

    def substep(source, target, step):
        def pair(p, carry):
            r = step + 2 * p
            for t in range(width // GROUP):
                at = pl.multiple_of(start_of(r) + GROUP * t, GROUP)
                f = [weights(at - GROUP + width * i) for i in range(2)]
                for h, out in enumerate(pair_of(source, at, f)):
                    for i in range(2):
                        target[h, pl.ds(at + width * i, GROUP), :] = out[i]
            return carry

        lax.fori_loop(0, (rows + 2 * (HALO - step)) // 2, pair, 0)

    buffers = [first, second]
    for step in range(1, SUBSTEPS):
        substep(buffers[(step - 1) % 2], buffers[step % 2], step)
    source = buffers[(SUBSTEPS - 1) % 2]
    gram[...] = jnp.zeros_like(gram)
    chunk = lines

    def last_chunk(q, carry):
        def pair(p, inner):
            r = q * chunk + 2 * p
            for t in range(0, lanes // GROUP, 2):
                parts = []
                for u in range(2):
                    at = start_of(HALO + r) + HALO + GROUP * (t + u)
                    f = [weights(at - GROUP + width * i) for i in range(2)]
                    parts.append(list(pair_of(source, at, f)))
                for i in range(2):
                    for h in range(halves):
                        both = jnp.concatenate([parts[0][h][i], parts[1][h][i]], axis=0).astype(BF16)
                        evolved[r + i, GROUP * t:GROUP * (t + 2), LANES * h:LANES * (h + 1)] = both
            return inner

        lax.fori_loop(0, chunk // 2, pair, 0)
        part = evolved[pl.ds(q * chunk, chunk)].reshape(chunk * lanes, fields)
        gram[...] += lax.dot_general(part, part, (((0,), (0,)), ((), ())), preferred_element_type=F32)
        storing(q).start()
        return carry

    lax.fori_loop(0, chunks, last_chunk, 0)
    h = fields // 2
    ri = lax.broadcasted_iota(jnp.int32, (h, h), 0)
    ci = lax.broadcasted_iota(jnp.int32, (h, h), 1)
    corner = gram[0:h, 0:h]
    payload[0:h] = jnp.where(ri <= ci, gram[h:2 * h, h:2 * h], corner)
    payload[h:2 * h] = gram[0:h, h:2 * h]
    diagonal = jnp.sum(jnp.where(ri == ci, corner, 0.0), axis=0, keepdims=True)
    payload[2 * h:] = jnp.broadcast_to(diagonal, (PACKED, h))
    for q in range(chunks):
        storing(q).wait()


def evolve(own, low, high, sides, table):
    rows, lanes, fields = own.shape
    width = lanes + 2 * HALO
    state = (fields // LANES, (rows + 2 * HALO) * width + 2 * GROUP, LANES)
    chunks = 8
    hbm, vmem = pl.BlockSpec(memory_space=pltpu.HBM), pl.BlockSpec(memory_space=pltpu.VMEM)
    return pl.pallas_call(
        evolve_kernel,
        in_specs=[hbm, vmem, vmem, vmem, vmem],
        out_specs=(hbm, vmem),
        out_shape=(
            pltpu.HBM((rows, lanes, fields), BF16),
            jax.ShapeDtypeStruct((fields + PACKED, fields // 2), F32),
        ),
        scratch_shapes=[
            pltpu.VMEM(state, F32),
            pltpu.VMEM(state, F32),
            pltpu.VMEM((3, table.shape[1] * LANES, LANES), F32),
            pltpu.VMEM((fields, fields), F32),
            pltpu.VMEM((rows, lanes, fields), BF16),
            pltpu.SemaphoreType.DMA((chunks,)),
            pltpu.SemaphoreType.DMA((chunks,)),
        ],
        compiler_params=pltpu.CompilerParams(vmem_limit_bytes=42 << 20),
    )(pltpu.with_memory_space_constraint(own, pltpu.HBM), low, high, sides, table)


def finish_kernel(total, pay, source, factor, exponents, basis, v, held, inverse, evolved, wide, out, read, write):
    rows, lanes, fields = evolved.shape
    chunks, step = out.shape[0], out.shape[2]
    pitch = step + 1

    def loading(q):
        return pltpu.make_async_copy(source.at[pl.ds(q * step, step)], evolved.at[pl.ds(q * step, step)], read.at[q])

    def storing(q):
        return pltpu.make_async_copy(out.at[q], basis.at[:, pl.ds(q * step, step)], write.at[q])

    for q in range(chunks):
        loading(q).start()
    factor_kernel(total, pay, factor, inverse, exponents, v, held)
    for q in range(chunks):
        loading(q).wait()
        for r in range(0, step, 2):
            cells = evolved[q * step + r:q * step + r + 2].reshape(2 * lanes, fields)
            part = lax.dot_general(inverse[...], cells, (((1,), (1,)), ((), ())), preferred_element_type=F32)
            for i in range(2):
                wide[pl.ds(r + i, fields, stride=pitch), :] = part[:, i * lanes:(i + 1) * lanes]

        def narrow(f, carry):
            out[q, f] = wide[pl.ds(f * pitch, step), :].astype(BF16)
            return carry

        lax.fori_loop(0, fields, narrow, 0, unroll=8)
        storing(q).start()
    for q in range(chunks):
        storing(q).wait()


def finish(pay, evolved, total):
    rows, lanes, fields = evolved.shape
    step = 16
    chunks = rows // step
    hbm, vmem = pl.BlockSpec(memory_space=pltpu.HBM), pl.BlockSpec(memory_space=pltpu.VMEM)
    return pl.pallas_call(
        functools.partial(finish_kernel, total),
        in_specs=[vmem, hbm],
        out_specs=(vmem, vmem, hbm),
        out_shape=(
            jax.ShapeDtypeStruct((fields, fields), F32),
            jax.ShapeDtypeStruct((1, fields), F32),
            jax.ShapeDtypeStruct((fields, rows, lanes), BF16),
        ),
        scratch_shapes=[
            pltpu.VMEM((3, LANES, LANES), F32),
            pltpu.VMEM((2 * GROUP * GROUP, LANES), F32),
            pltpu.VMEM((fields, fields), BF16),
            pltpu.VMEM((rows, lanes, fields), BF16),
            pltpu.VMEM(((step + 1) * fields, lanes), F32),
            pltpu.VMEM((chunks, fields, step, lanes), BF16),
            pltpu.SemaphoreType.DMA((chunks,)),
            pltpu.SemaphoreType.DMA((chunks,)),
        ],
        compiler_params=pltpu.CompilerParams(vmem_limit_bytes=24 << 20),
    )(pay, pltpu.with_memory_space_constraint(evolved, pltpu.HBM))


def shifted(block, down, right):
    nx, ny = lax.axis_size("gx"), lax.axis_size("gy")
    pairs = []
    for x in range(nx):
        for y in range(ny):
            pairs.append((x * ny + y, (x + down) % nx * ny + (y + right) % ny))
    return lax.ppermute(block, ("gx", "gy"), pairs)


def swapped(block, axis, bit):
    return lax.ppermute(block, axis, [(i, i ^ bit) for i in range(lax.axis_size(axis))])


def summed(payload):
    nx, ny = lax.axis_size("gx"), lax.axis_size("gy")
    if nx & (nx - 1) or ny & (ny - 1) or nx < 2:
        return lax.psum(payload, ("gx", "gy"))
    half = payload.shape[0] // 2
    side = lax.axis_index("gx") % 2
    kept = lax.dynamic_slice_in_dim(payload, side * half, half, 0)
    given = lax.dynamic_slice_in_dim(payload, (1 - side) * half, half, 0)
    total = kept + swapped(given, "gx", 1)
    for axis, bits in (("gy", range(ny.bit_length() - 1)), ("gx", range(1, nx.bit_length() - 1))):
        for bit in bits:
            total = total + swapped(total, axis, 1 << bit)
    other = swapped(total, "gx", 1)
    return jnp.where(side == 0, jnp.concatenate([total, other]), jnp.concatenate([other, total]))


def pieces(block):
    out = []
    for _ in range(3):
        part = lax.reduce_precision(block, 8, 7)
        out.append(part.astype(BF16))
        block = block - part
    return jnp.concatenate(out)


def joined(parts):
    count = parts.shape[0] // 3
    wide = parts.astype(F32)
    return wide[:count] + wide[count:2 * count] + wide[2 * count:]


def tail_of(parts, fields):
    flat = parts.reshape(-1)
    return jnp.pad(flat, (0, -flat.size % (PACKED * fields))).reshape(-1, fields)


def unloaded(matrix, rows, cols):
    cells = rows * cols
    parts = matrix[cells:].reshape(-1)[:9 * cells].reshape(9, rows, cols)
    return matrix[:cells].reshape(rows, cols, -1), parts


def per_device(tangent, courant_x, courant_y, growth):
    fields, rows, cols = tangent.shape
    nx, ny = lax.axis_size("gx"), lax.axis_size("gy")
    block = jnp.stack([courant_x, courant_y, growth])
    parts = pieces(block)

    def edges(x, axis):
        size = x.shape[axis]
        return lax.slice_in_dim(x, size - HALO, size, axis=axis), lax.slice_in_dim(x, 0, HALO, axis=axis)

    part_last, part_begin = edges(parts, 1)
    part_side = jnp.concatenate(edges(parts, 2), axis=2)
    own, last, begin, both = turn(tangent, [tail_of(part, fields) for part in (part_last, part_begin, part_side)])
    low = unloaded(shifted(last, 1, 0), HALO, cols)
    high = unloaded(shifted(begin, -1, 0), HALO, cols)
    side, side_part = unloaded(shifted(both, 0, 1), rows, 2 * HALO)
    if ny > 2:
        east, east_part = unloaded(shifted(both, 0, -1), rows, 2 * HALO)
        side = jnp.concatenate([side[:, :HALO], east[:, HALO:]], axis=1)
        side_part = jnp.concatenate([side_part[:, :, :HALO], east_part[:, :, HALO:]], axis=2)

    def corner(state, part, down):
        matrix = jnp.concatenate([state.reshape(-1, fields), tail_of(part, fields)])
        return unloaded(shifted(matrix, down, 0), HALO, 2 * HALO)

    state_last, state_begin = edges(side, 0)
    part_last, part_begin = edges(side_part, 1)
    low_side = corner(state_last, part_last, 1)
    high_side = corner(state_begin, part_begin, -1)
    sides = jnp.concatenate([low_side[0], side, high_side[0]])
    middle = jnp.concatenate([joined(low[1]), block, joined(high[1])], axis=1)
    around = joined(jnp.concatenate([low_side[1], side_part, high_side[1]], axis=1))
    table = jnp.concatenate([around[:, :, :HALO], middle, around[:, :, HALO:]], axis=2).reshape(3, -1)
    table = jnp.pad(table, ((0, 0), (0, -table.shape[1] % LANES))).reshape(3, -1, LANES)
    evolved, payload = evolve(own, low[0], high[0], sides, table)
    total = float(rows * nx * cols * ny)
    factor, exponents, basis = finish(summed(payload), evolved, total)
    return basis, factor, exponents.reshape(fields)


def solution(mesh):
    placed = (P(None, "gx", "gy"), P("gx", "gy"), P("gx", "gy"), P("gx", "gy"))
    return jax.shard_map(
        per_device,
        mesh=mesh,
        in_specs=placed,
        out_specs=(P(None, "gx", "gy"), P(), P()),
        check_vma=False,
    )
```

```python
import functools

import jax
import jax.numpy as jnp
from jax import lax
from jax.experimental import pallas as pl
from jax.experimental.pallas import tpu as pltpu
from jax.sharding import PartitionSpec as P

F32 = jnp.float32
BF16 = jnp.bfloat16
SUBSTEPS = 4
LANES = 128
HALO = SUBSTEPS
GROUP = 8
EDGE = 2 * HALO
PACKED = 16
TALL = 4


def tree(terms):
    while len(terms) > 1:
        terms = [a + b for a, b in zip(terms[::2], terms[1::2])] + terms[len(terms) & ~1:]
    return terms[0]


def spread(ref, *at):
    *block, row = at
    return ref[(*block, pl.ds(row, GROUP, stride=0), slice(None))]


def factor_block(v, held):
    sub = lax.broadcasted_iota(jnp.int32, (8, 128), 0)
    n = 8
    for p in range(16):
        c0 = p * n
        diag = v[0, c0:c0 + n]
        column = [jnp.broadcast_to(diag[:, c0 + j:c0 + j + 1], (n, 128)) for j in range(n)]
        base = p % 2 * n * n
        for j in range(n):
            held[base + n * j:base + n * (j + 1)] = column[j]
        d = {(i, j): spread(held, base + n * j + i) for j in range(n) for i in range(j + 1)}
        inv, r, x = {}, {}, {}
        for j in range(n):
            inv[j] = lax.rsqrt(d[j, j])
            for k in range(j + 1, n):
                r[j, k] = d[j, k] * inv[j]
            for i in range(j + 1, n):
                for k in range(i, n):
                    d[i, k] = d[i, k] - r[j, i] * r[j, k]
        for j in range(n):
            x[j, j] = inv[j]
            for i in range(j + 1, n):
                x[i, j] = -(inv[i] * tree([r[k, i] * x[k, j] for k in range(j, i)]))
        dinv = {}
        for a in range(n):
            for b in range(a, n):
                dinv[a, b] = dinv[b, a] = tree([x[m, a] * x[m, b] for m in range(b, n)])
        ys = []
        for t in range(3):
            rows = [spread(v, t, c0 + k) for k in range(n)]
            ys.append([tree([dinv[a, k] * rows[k] for k in range(n)]) for a in range(n)])
            out = x[0, 0] * rows[0]
            for i in range(1, n):
                out = jnp.where(sub == i, tree([x[i, k] * rows[k] for k in range(i + 1)]), out)
            v[t, c0:c0 + n] = out
        for g in range(p + 1, 16):
            ag = v[0, n * g:n * g + n]
            ab = [jnp.broadcast_to(ag[:, c0 + j:c0 + j + 1], (n, 128)) for j in range(n)]
            for t in range(3):
                v[t, n * g:n * g + n] = v[t, n * g:n * g + n] - tree([ab[j] * ys[t][j] for j in range(n)])

def dot_t(a, b):
    return lax.dot_general(a, b, (((0,), (0,)), ((), ())), precision=lax.Precision.HIGHEST, preferred_element_type=F32)

def factor_kernel(total, pay, factor, inverse, exponents, v, held):
    h = 128
    ri = lax.broadcasted_iota(jnp.int32, (h, h), 0)
    ci = lax.broadcasted_iota(jnp.int32, (h, h), 1)
    eye = jnp.where(ri == ci, 1.0, 0.0).astype(F32)
    fold = pay[0:h, :] / total
    turned = fold.T
    diag0 = jnp.broadcast_to(pay[2 * h:2 * h + 1, :], (h, h)) / total
    v[0] = jnp.where(ri == ci, diag0, jnp.where(ri < ci, turned, fold))
    v[1] = pay[h:2 * h, :] / total
    v[2] = eye
    rest = jnp.where(ri <= ci, fold, turned)
    factor_block(v, held)
    r00 = jnp.where(ri <= ci, v[0], 0.0)
    r01 = v[1]
    l00 = jnp.where(ri >= ci, v[2], 0.0)
    factor[0:h, 0:h] = r00
    factor[0:h, h:2 * h] = r01
    inverse[0:h, 0:h] = l00.astype(jnp.bfloat16)
    inverse[0:h, h:2 * h] = jnp.zeros((h, h), jnp.bfloat16)
    exponents[:, 0:h] = jnp.log(jnp.sum(r00 * eye, axis=0, keepdims=True))
    v[0] = rest - dot_t(r01, r01)
    v[1] = -dot_t(r01, l00)
    v[2] = eye
    factor_block(v, held)
    r11 = jnp.where(ri <= ci, v[0], 0.0)
    factor[h:2 * h, 0:h] = jnp.zeros((h, h), F32)
    factor[h:2 * h, h:2 * h] = r11
    inverse[h:2 * h, 0:h] = v[1].astype(jnp.bfloat16)
    inverse[h:2 * h, h:2 * h] = jnp.where(ri >= ci, v[2], 0.0).astype(jnp.bfloat16)
    exponents[:, h:2 * h] = jnp.log(jnp.sum(r11 * eye, axis=0, keepdims=True))


def turn_kernel(source, low_tail, high_tail, side_tail, target, last, begin, side, tangent, wide, turned, read, write):
    chunks, fields, lines, lanes = tangent.shape
    rows = chunks * lines
    pitch = lines + 1

    def loading(q):
        return pltpu.make_async_copy(source.at[:, pl.ds(q * lines, lines)], tangent.at[q], read.at[q])

    def storing(q):
        return pltpu.make_async_copy(turned.at[pl.ds(q * lines, lines)], target.at[pl.ds(q * lines, lines)], write.at[q])

    for q in range(chunks):
        loading(q).start()
    for q in range(chunks):
        loading(q).wait()

        def widen(f, carry):
            wide[pl.ds(f * pitch, lines), :] = tangent[q, f].astype(F32)
            return carry

        lax.fori_loop(0, fields, widen, 0, unroll=16)

        def turn_rows(p, carry):
            ends = []
            for i in range(2):
                line = wide[pl.ds(2 * p + i, fields, stride=pitch), :].T
                turned[q * lines + 2 * p + i] = line.astype(BF16)
                ends += [line[lanes - HALO:], line[:HALO]]
            at = pl.multiple_of((q * lines + 2 * p) * 2 * HALO, 4 * HALO)
            side[pl.ds(at, 4 * HALO), :] = jnp.concatenate(ends).astype(BF16)
            return carry

        lax.fori_loop(0, lines // 2, turn_rows, 0, unroll=2)
        storing(q).start()
    count = HALO * lanes
    last[0:count] = turned[rows - HALO:].reshape(count, fields)
    last[count:] = low_tail[...]
    begin[0:count] = turned[:HALO].reshape(count, fields)
    begin[count:] = high_tail[...]
    side[2 * HALO * rows:] = side_tail[...]
    for q in range(chunks):
        storing(q).wait()


def turn(tangent, tails):
    fields, rows, lanes = tangent.shape
    lines = 16
    chunks = rows // lines
    hbm, vmem = pl.BlockSpec(memory_space=pltpu.HBM), pl.BlockSpec(memory_space=pltpu.VMEM)
    matrix = [jax.ShapeDtypeStruct((cells + tail.shape[0], fields), BF16)
              for cells, tail in zip((HALO * lanes, HALO * lanes, 2 * HALO * rows), tails)]
    return pl.pallas_call(
        turn_kernel,
        in_specs=[hbm, vmem, vmem, vmem],
        out_specs=(hbm, vmem, vmem, vmem),
        out_shape=(pltpu.HBM((rows, lanes, fields), BF16), *matrix),
        scratch_shapes=[
            pltpu.VMEM((chunks, fields, lines, lanes), BF16),
            pltpu.VMEM((fields * (lines + 1), lanes), F32),
            pltpu.VMEM((rows, lanes, fields), BF16),
            pltpu.SemaphoreType.DMA((chunks,)),
            pltpu.SemaphoreType.DMA((chunks,)),
        ],
        compiler_params=pltpu.CompilerParams(vmem_limit_bytes=24 << 20),
    )(pltpu.with_memory_space_constraint(tangent, pltpu.HBM), *tails)


def evolve_kernel(source_block, low, high, sides, table, target_block, payload, first, second, coef, gram, own, read, write):
    rows, lanes, fields = own.shape
    evolved = own
    chunks = read.shape[0]
    lines = rows // chunks

    def loading(q):
        return pltpu.make_async_copy(source_block.at[pl.ds(q * lines, lines)], own.at[pl.ds(q * lines, lines)], read.at[q])

    def storing(q):
        return pltpu.make_async_copy(
            evolved.at[pl.ds(q * lines, lines)], target_block.at[pl.ds(q * lines, lines)], write.at[q])

    for q in range(chunks):
        loading(q).start()
    width = lanes + 2 * HALO
    halves = fields // LANES
    start_of = lambda r: GROUP + r * width

    for m in range(3):
        turned_table = jnp.concatenate([table[m], jnp.zeros((LANES - table.shape[1], LANES), F32)]).T
        for q in range(table.shape[1]):
            coef[m, LANES * q:LANES * (q + 1), :] = jnp.broadcast_to(turned_table[:, q:q + 1], (LANES, LANES))

    def fill(row, block):
        for h in range(halves):
            first[h, pl.ds(start_of(row) + HALO, lanes), :] = block[:, LANES * h:LANES * (h + 1)].astype(F32)

    for i in range(HALO):
        fill(i, low[i])
        fill(HALO + rows + i, high[i])

    def fill_own(r, carry):
        fill(HALO + r, own[r])
        return carry

    for q in range(chunks):
        loading(q).wait()
        lax.fori_loop(q * lines, (q + 1) * lines, fill_own, 0, unroll=2)

    def fill_sides(r, carry):
        pair = sides[r].astype(F32)
        for h in range(halves):
            first[h, pl.ds(start_of(r), HALO), :] = pair[:HALO, LANES * h:LANES * (h + 1)]
            first[h, pl.ds(start_of(r) + HALO + lanes, HALO), :] = pair[HALO:, LANES * h:LANES * (h + 1)]
        return carry

    lax.fori_loop(0, rows + 2 * HALO, fill_sides, 0, unroll=4)

    def weights(at):
        north, east, centre = [coef[m, pl.ds(at, GROUP), :] for m in range(3)]
        return centre, north, 0.4 - north, east, 0.4 - east

    def combine(f, c, n, s, e, w):
        return f[0] * c + (f[1] * n + f[2] * s) + (f[3] * e + f[4] * w)

    def advanced(source, at, f):
        count = len(f)
        for h in range(halves):
            value = [source[h, pl.ds(at + width * i, GROUP), :] for i in range(-1, count + 1)]
            east = [source[h, pl.ds(at + width * i + 1, GROUP), :] for i in range(count)]
            west = [source[h, pl.ds(at + width * i - 1, GROUP), :] for i in range(count)]
            yield [combine(f[i], value[i + 1], value[i + 2], value[i], east[i], west[i]) for i in range(count)]

    def substep(source, target, step):
        def some_rows(r, count):
            for t in range(width // GROUP):
                at = pl.multiple_of(start_of(r) + GROUP * t, GROUP)
                f = [weights(at - GROUP + width * i) for i in range(count)]
                for h, out in enumerate(advanced(source, at, f)):
                    for i in range(count):
                        target[h, pl.ds(at + width * i, GROUP), :] = out[i]

        def block(p, carry):
            some_rows(step + TALL * p, TALL)
            return carry

        count = rows + 2 * (HALO - step)
        lax.fori_loop(0, count // TALL, block, 0)
        if count % TALL:
            some_rows(step + count // TALL * TALL, count % TALL)

    buffers = [first, second]
    for step in range(1, SUBSTEPS):
        substep(buffers[(step - 1) % 2], buffers[step % 2], step)
    source = buffers[(SUBSTEPS - 1) % 2]
    gram[...] = jnp.zeros_like(gram)
    chunk = lines

    def last_chunk(q, carry):
        def block(p, inner):
            r = q * chunk + TALL * p
            for t in range(0, lanes // GROUP, 2):
                parts = []
                for u in range(2):
                    at = start_of(HALO + r) + HALO + GROUP * (t + u)
                    f = [weights(at - GROUP + width * i) for i in range(TALL)]
                    parts.append(list(advanced(source, at, f)))
                for i in range(TALL):
                    for h in range(halves):
                        both = jnp.concatenate([parts[0][h][i], parts[1][h][i]], axis=0).astype(BF16)
                        evolved[r + i, GROUP * t:GROUP * (t + 2), LANES * h:LANES * (h + 1)] = both
            return inner

        lax.fori_loop(0, chunk // TALL, block, 0)
        part = evolved[pl.ds(q * chunk, chunk)].reshape(chunk * lanes, fields)
        gram[...] += lax.dot_general(part, part, (((0,), (0,)), ((), ())), preferred_element_type=F32)
        storing(q).start()
        return carry

    lax.fori_loop(0, chunks, last_chunk, 0)
    h = fields // 2
    ri = lax.broadcasted_iota(jnp.int32, (h, h), 0)
    ci = lax.broadcasted_iota(jnp.int32, (h, h), 1)
    corner = gram[0:h, 0:h]
    payload[0:h] = jnp.where(ri <= ci, gram[h:2 * h, h:2 * h], corner)
    payload[h:2 * h] = gram[0:h, h:2 * h]
    diagonal = jnp.sum(jnp.where(ri == ci, corner, 0.0), axis=0, keepdims=True)
    payload[2 * h:] = jnp.broadcast_to(diagonal, (PACKED, h))
    for q in range(chunks):
        storing(q).wait()


def evolve(own, low, high, sides, table):
    rows, lanes, fields = own.shape
    width = lanes + 2 * HALO
    state = (fields // LANES, (rows + 2 * HALO) * width + 2 * GROUP, LANES)
    chunks = 8
    hbm, vmem = pl.BlockSpec(memory_space=pltpu.HBM), pl.BlockSpec(memory_space=pltpu.VMEM)
    return pl.pallas_call(
        evolve_kernel,
        in_specs=[hbm, vmem, vmem, vmem, vmem],
        out_specs=(hbm, vmem),
        out_shape=(
            pltpu.HBM((rows, lanes, fields), BF16),
            jax.ShapeDtypeStruct((fields + PACKED, fields // 2), F32),
        ),
        scratch_shapes=[
            pltpu.VMEM(state, F32),
            pltpu.VMEM(state, F32),
            pltpu.VMEM((3, table.shape[1] * LANES, LANES), F32),
            pltpu.VMEM((fields, fields), F32),
            pltpu.VMEM((rows, lanes, fields), BF16),
            pltpu.SemaphoreType.DMA((chunks,)),
            pltpu.SemaphoreType.DMA((chunks,)),
        ],
        compiler_params=pltpu.CompilerParams(vmem_limit_bytes=42 << 20),
    )(pltpu.with_memory_space_constraint(own, pltpu.HBM), low, high, sides, table)


def finish_kernel(total, pay, source, factor, exponents, basis, v, held, inverse, evolved, wide, out, read, write):
    rows, lanes, fields = evolved.shape
    chunks, step = out.shape[0], out.shape[2]
    pitch = step + 1

    def loading(q):
        return pltpu.make_async_copy(source.at[pl.ds(q * step, step)], evolved.at[pl.ds(q * step, step)], read.at[q])

    def storing(q):
        return pltpu.make_async_copy(out.at[q], basis.at[:, pl.ds(q * step, step)], write.at[q])

    for q in range(chunks):
        loading(q).start()
    factor_kernel(total, pay, factor, inverse, exponents, v, held)
    for q in range(chunks):
        loading(q).wait()
        for r in range(0, step, 2):
            cells = evolved[q * step + r:q * step + r + 2].reshape(2 * lanes, fields)
            part = lax.dot_general(inverse[...], cells, (((1,), (1,)), ((), ())), preferred_element_type=F32)
            for i in range(2):
                wide[pl.ds(r + i, fields, stride=pitch), :] = part[:, i * lanes:(i + 1) * lanes]

        def narrow(f, carry):
            out[q, f] = wide[pl.ds(f * pitch, step), :].astype(BF16)
            return carry

        lax.fori_loop(0, fields, narrow, 0, unroll=64)
        storing(q).start()
    for q in range(chunks):
        storing(q).wait()


def finish(pay, evolved, total):
    rows, lanes, fields = evolved.shape
    step = 16
    chunks = rows // step
    hbm, vmem = pl.BlockSpec(memory_space=pltpu.HBM), pl.BlockSpec(memory_space=pltpu.VMEM)
    return pl.pallas_call(
        functools.partial(finish_kernel, total),
        in_specs=[vmem, hbm],
        out_specs=(vmem, vmem, hbm),
        out_shape=(
            jax.ShapeDtypeStruct((fields, fields), F32),
            jax.ShapeDtypeStruct((1, fields), F32),
            jax.ShapeDtypeStruct((fields, rows, lanes), BF16),
        ),
        scratch_shapes=[
            pltpu.VMEM((3, LANES, LANES), F32),
            pltpu.VMEM((2 * GROUP * GROUP, LANES), F32),
            pltpu.VMEM((fields, fields), BF16),
            pltpu.VMEM((rows, lanes, fields), BF16),
            pltpu.VMEM(((step + 1) * fields, lanes), F32),
            pltpu.VMEM((chunks, fields, step, lanes), BF16),
            pltpu.SemaphoreType.DMA((chunks,)),
            pltpu.SemaphoreType.DMA((chunks,)),
        ],
        compiler_params=pltpu.CompilerParams(vmem_limit_bytes=24 << 20),
    )(pay, pltpu.with_memory_space_constraint(evolved, pltpu.HBM))


def shifted(block, down, right):
    nx, ny = lax.axis_size("gx"), lax.axis_size("gy")
    pairs = []
    for x in range(nx):
        for y in range(ny):
            pairs.append((x * ny + y, (x + down) % nx * ny + (y + right) % ny))
    return lax.ppermute(block, ("gx", "gy"), pairs)


def swapped(block, axis, bit):
    return lax.ppermute(block, axis, [(i, i ^ bit) for i in range(lax.axis_size(axis))])


def summed(payload):
    nx, ny = lax.axis_size("gx"), lax.axis_size("gy")
    if nx & (nx - 1) or ny & (ny - 1) or nx < 2:
        return lax.psum(payload, ("gx", "gy"))
    half = payload.shape[0] // 2
    side = lax.axis_index("gx") % 2
    kept = lax.dynamic_slice_in_dim(payload, side * half, half, 0)
    given = lax.dynamic_slice_in_dim(payload, (1 - side) * half, half, 0)
    total = kept + swapped(given, "gx", 1)
    for axis, bits in (("gy", range(ny.bit_length() - 1)), ("gx", range(1, nx.bit_length() - 1))):
        for bit in bits:
            total = total + swapped(total, axis, 1 << bit)
    other = swapped(total, "gx", 1)
    return jnp.where(side == 0, jnp.concatenate([total, other]), jnp.concatenate([other, total]))


def pieces(block):
    out = []
    for _ in range(3):
        part = lax.reduce_precision(block, 8, 7)
        out.append(part.astype(BF16))
        block = block - part
    return jnp.concatenate(out)


def joined(parts):
    count = parts.shape[0] // 3
    wide = parts.astype(F32)
    return wide[:count] + wide[count:2 * count] + wide[2 * count:]


def tail_of(parts, fields):
    flat = parts.reshape(-1)
    return jnp.pad(flat, (0, -flat.size % (PACKED * fields))).reshape(-1, fields)


def unloaded(matrix, rows, cols):
    cells = rows * cols
    parts = matrix[cells:].reshape(-1)[:9 * cells].reshape(9, rows, cols)
    return matrix[:cells].reshape(rows, cols, -1), parts


def per_device(tangent, courant_x, courant_y, growth):
    fields, rows, cols = tangent.shape
    nx, ny = lax.axis_size("gx"), lax.axis_size("gy")
    block = jnp.stack([courant_x, courant_y, growth])
    parts = pieces(block)

    def edges(x, axis):
        size = x.shape[axis]
        return lax.slice_in_dim(x, size - HALO, size, axis=axis), lax.slice_in_dim(x, 0, HALO, axis=axis)

    part_last, part_begin = edges(parts, 1)
    part_side = jnp.concatenate(edges(parts, 2), axis=2)
    own, last, begin, both = turn(tangent, [tail_of(part, fields) for part in (part_last, part_begin, part_side)])
    low = unloaded(shifted(last, 1, 0), HALO, cols)
    high = unloaded(shifted(begin, -1, 0), HALO, cols)
    side, side_part = unloaded(shifted(both, 0, 1), rows, 2 * HALO)
    if ny > 2:
        east, east_part = unloaded(shifted(both, 0, -1), rows, 2 * HALO)
        side = jnp.concatenate([side[:, :HALO], east[:, HALO:]], axis=1)
        side_part = jnp.concatenate([side_part[:, :, :HALO], east_part[:, :, HALO:]], axis=2)

    def corner(state, part, down):
        matrix = jnp.concatenate([state.reshape(-1, fields), tail_of(part, fields)])
        return unloaded(shifted(matrix, down, 0), HALO, 2 * HALO)

    state_last, state_begin = edges(side, 0)
    part_last, part_begin = edges(side_part, 1)
    low_side = corner(state_last, part_last, 1)
    high_side = corner(state_begin, part_begin, -1)
    sides = jnp.concatenate([low_side[0], side, high_side[0]])
    middle = jnp.concatenate([joined(low[1]), block, joined(high[1])], axis=1)
    around = joined(jnp.concatenate([low_side[1], side_part, high_side[1]], axis=1))
    table = jnp.concatenate([around[:, :, :HALO], middle, around[:, :, HALO:]], axis=2)
    table = jnp.stack([0.2 - table[0], 0.2 - table[1], 0.2 + table[2]]).reshape(3, -1)
    table = jnp.pad(table, ((0, 0), (0, -table.shape[1] % LANES))).reshape(3, -1, LANES)
    evolved, payload = evolve(own, low[0], high[0], sides, table)
    total = float(rows * nx * cols * ny)
    factor, exponents, basis = finish(summed(payload), evolved, total)
    return basis, factor, exponents.reshape(fields)


def solution(mesh):
    placed = (P(None, "gx", "gy"), P("gx", "gy"), P("gx", "gy"), P("gx", "gy"))
    return jax.shard_map(
        per_device,
        mesh=mesh,
        in_specs=placed,
        out_specs=(P(None, "gx", "gy"), P(), P()),
        check_vma=False,
    )
```

```python
import functools

import jax
import jax.numpy as jnp
from jax import lax
from jax.experimental import pallas as pl
from jax.experimental.pallas import tpu as pltpu
from jax.sharding import PartitionSpec as P

F32 = jnp.float32
BF16 = jnp.bfloat16
SUBSTEPS = 4
LANES = 128
HALO = SUBSTEPS
GROUP = 8
EDGE = 2 * HALO
PACKED = 16
TALL = 4


def tree(terms):
    while len(terms) > 1:
        terms = [a + b for a, b in zip(terms[::2], terms[1::2])] + terms[len(terms) & ~1:]
    return terms[0]


def spread(ref, *at):
    *block, row = at
    return ref[(*block, pl.ds(row, GROUP, stride=0), slice(None))]


def factor_block(v, held):
    sub = lax.broadcasted_iota(jnp.int32, (8, 128), 0)
    n = 8
    for p in range(16):
        c0 = p * n
        diag = v[0, c0:c0 + n]
        column = [jnp.broadcast_to(diag[:, c0 + j:c0 + j + 1], (n, 128)) for j in range(n)]
        base = p % 2 * n * n
        for j in range(n):
            held[base + n * j:base + n * (j + 1)] = column[j]
        d = {(i, j): spread(held, base + n * j + i) for j in range(n) for i in range(j + 1)}
        inv, r, x = {}, {}, {}
        for j in range(n):
            inv[j] = lax.rsqrt(d[j, j])
            for k in range(j + 1, n):
                r[j, k] = d[j, k] * inv[j]
            for i in range(j + 1, n):
                for k in range(i, n):
                    d[i, k] = d[i, k] - r[j, i] * r[j, k]
        for j in range(n):
            x[j, j] = inv[j]
            for i in range(j + 1, n):
                x[i, j] = -(inv[i] * tree([r[k, i] * x[k, j] for k in range(j, i)]))
        dinv = {}
        for a in range(n):
            for b in range(a, n):
                dinv[a, b] = dinv[b, a] = tree([x[m, a] * x[m, b] for m in range(b, n)])
        ys = []
        for t in range(3):
            rows = [spread(v, t, c0 + k) for k in range(n)]
            ys.append([tree([dinv[a, k] * rows[k] for k in range(n)]) for a in range(n)])
            out = x[0, 0] * rows[0]
            for i in range(1, n):
                out = jnp.where(sub == i, tree([x[i, k] * rows[k] for k in range(i + 1)]), out)
            v[t, c0:c0 + n] = out
        for g in range(p + 1, 16):
            ag = v[0, n * g:n * g + n]
            ab = [jnp.broadcast_to(ag[:, c0 + j:c0 + j + 1], (n, 128)) for j in range(n)]
            for t in range(3):
                v[t, n * g:n * g + n] = v[t, n * g:n * g + n] - tree([ab[j] * ys[t][j] for j in range(n)])

def dot_t(a, b):
    return lax.dot_general(a, b, (((0,), (0,)), ((), ())), precision=lax.Precision.HIGHEST, preferred_element_type=F32)

def factor_kernel(total, pay, factor, inverse, exponents, v, held):
    h = 128
    ri = lax.broadcasted_iota(jnp.int32, (h, h), 0)
    ci = lax.broadcasted_iota(jnp.int32, (h, h), 1)
    eye = jnp.where(ri == ci, 1.0, 0.0).astype(F32)
    fold = pay[0:h, :] / total
    turned = fold.T
    diag0 = jnp.broadcast_to(pay[2 * h:2 * h + 1, :], (h, h)) / total
    v[0] = jnp.where(ri == ci, diag0, jnp.where(ri < ci, turned, fold))
    v[1] = pay[h:2 * h, :] / total
    v[2] = eye
    rest = jnp.where(ri <= ci, fold, turned)
    factor_block(v, held)
    r00 = jnp.where(ri <= ci, v[0], 0.0)
    r01 = v[1]
    l00 = jnp.where(ri >= ci, v[2], 0.0)
    factor[0:h, 0:h] = r00
    factor[0:h, h:2 * h] = r01
    inverse[0:h, 0:h] = l00.astype(jnp.bfloat16)
    inverse[0:h, h:2 * h] = jnp.zeros((h, h), jnp.bfloat16)
    exponents[:, 0:h] = jnp.log(jnp.sum(r00 * eye, axis=0, keepdims=True))
    v[0] = rest - dot_t(r01, r01)
    v[1] = -dot_t(r01, l00)
    v[2] = eye
    factor_block(v, held)
    r11 = jnp.where(ri <= ci, v[0], 0.0)
    factor[h:2 * h, 0:h] = jnp.zeros((h, h), F32)
    factor[h:2 * h, h:2 * h] = r11
    inverse[h:2 * h, 0:h] = v[1].astype(jnp.bfloat16)
    inverse[h:2 * h, h:2 * h] = jnp.where(ri >= ci, v[2], 0.0).astype(jnp.bfloat16)
    exponents[:, h:2 * h] = jnp.log(jnp.sum(r11 * eye, axis=0, keepdims=True))


def turn_kernel(source, low_tail, high_tail, side_tail, target, last, begin, side, tangent, wide, turned, read, write):
    chunks, fields, lines, lanes = tangent.shape
    rows = chunks * lines
    pitch = lines + 1

    def loading(q):
        return pltpu.make_async_copy(source.at[:, pl.ds(q * lines, lines)], tangent.at[q], read.at[q])

    def storing(q):
        return pltpu.make_async_copy(turned.at[pl.ds(q * lines, lines)], target.at[pl.ds(q * lines, lines)], write.at[q])

    for q in range(chunks):
        loading(q).start()
    for q in range(chunks):
        loading(q).wait()

        def widen(f, carry):
            wide[pl.ds(f * pitch, lines), :] = tangent[q, f].astype(F32)
            return carry

        lax.fori_loop(0, fields, widen, 0, unroll=16)

        def turn_rows(p, carry):
            ends = []
            for i in range(2):
                line = wide[pl.ds(2 * p + i, fields, stride=pitch), :].T
                turned[q * lines + 2 * p + i] = line.astype(BF16)
                ends += [line[lanes - HALO:], line[:HALO]]
            at = pl.multiple_of((q * lines + 2 * p) * 2 * HALO, 4 * HALO)
            side[pl.ds(at, 4 * HALO), :] = jnp.concatenate(ends).astype(BF16)
            return carry

        lax.fori_loop(0, lines // 2, turn_rows, 0, unroll=2)
        storing(q).start()
    count = HALO * lanes
    last[0:count] = turned[rows - HALO:].reshape(count, fields)
    last[count:] = low_tail[...]
    begin[0:count] = turned[:HALO].reshape(count, fields)
    begin[count:] = high_tail[...]
    side[2 * HALO * rows:] = side_tail[...]
    for q in range(chunks):
        storing(q).wait()


def turn(tangent, tails):
    fields, rows, lanes = tangent.shape
    lines = 16
    chunks = rows // lines
    hbm, vmem = pl.BlockSpec(memory_space=pltpu.HBM), pl.BlockSpec(memory_space=pltpu.VMEM)
    matrix = [jax.ShapeDtypeStruct((cells + tail.shape[0], fields), BF16)
              for cells, tail in zip((HALO * lanes, HALO * lanes, 2 * HALO * rows), tails)]
    return pl.pallas_call(
        turn_kernel,
        in_specs=[hbm, vmem, vmem, vmem],
        out_specs=(hbm, vmem, vmem, vmem),
        out_shape=(pltpu.HBM((rows, lanes, fields), BF16), *matrix),
        scratch_shapes=[
            pltpu.VMEM((chunks, fields, lines, lanes), BF16),
            pltpu.VMEM((fields * (lines + 1), lanes), F32),
            pltpu.VMEM((rows, lanes, fields), BF16),
            pltpu.SemaphoreType.DMA((chunks,)),
            pltpu.SemaphoreType.DMA((chunks,)),
        ],
        compiler_params=pltpu.CompilerParams(vmem_limit_bytes=24 << 20),
    )(pltpu.with_memory_space_constraint(tangent, pltpu.HBM), *tails)


def evolve_kernel(source_block, low, high, sides, table, target_block, payload, first, second, coef, gram, own, read, write):
    rows, lanes, fields = own.shape
    evolved = own
    chunks = read.shape[0]
    lines = rows // chunks

    def loading(q):
        return pltpu.make_async_copy(source_block.at[pl.ds(q * lines, lines)], own.at[pl.ds(q * lines, lines)], read.at[q])

    def storing(q):
        return pltpu.make_async_copy(
            evolved.at[pl.ds(q * lines, lines)], target_block.at[pl.ds(q * lines, lines)], write.at[q])

    for q in range(chunks):
        loading(q).start()
    width = lanes + 2 * HALO
    halves = fields // LANES
    start_of = lambda r: GROUP + r * width

    for m in range(3):
        line = 0.2 + table[m] if m == 2 else 0.2 - table[m]
        turned_table = jnp.concatenate([line, jnp.zeros((LANES - table.shape[1], LANES), F32)]).T
        for q in range(table.shape[1]):
            coef[m, LANES * q:LANES * (q + 1), :] = jnp.broadcast_to(turned_table[:, q:q + 1], (LANES, LANES))

    def fill(row, block):
        for h in range(halves):
            first[h, pl.ds(start_of(row) + HALO, lanes), :] = block[:, LANES * h:LANES * (h + 1)].astype(F32)

    for i in range(HALO):
        fill(i, low[i])
        fill(HALO + rows + i, high[i])

    def fill_own(r, carry):
        fill(HALO + r, own[r])
        return carry

    for q in range(chunks):
        loading(q).wait()
        lax.fori_loop(q * lines, (q + 1) * lines, fill_own, 0, unroll=2)

    def fill_sides(r, carry):
        pair = sides[r].astype(F32)
        for h in range(halves):
            first[h, pl.ds(start_of(r), HALO), :] = pair[:HALO, LANES * h:LANES * (h + 1)]
            first[h, pl.ds(start_of(r) + HALO + lanes, HALO), :] = pair[HALO:, LANES * h:LANES * (h + 1)]
        return carry

    lax.fori_loop(0, rows + 2 * HALO, fill_sides, 0, unroll=4)

    def weights(at):
        north, east, centre = [coef[m, pl.ds(at, GROUP), :] for m in range(3)]
        return centre, north, 0.4 - north, east, 0.4 - east

    def combine(f, c, n, s, e, w):
        return f[0] * c + (f[1] * n + f[2] * s) + (f[3] * e + f[4] * w)

    def advanced(source, at, f):
        count = len(f)
        for h in range(halves):
            value = [source[h, pl.ds(at + width * i, GROUP), :] for i in range(-1, count + 1)]
            east = [source[h, pl.ds(at + width * i + 1, GROUP), :] for i in range(count)]
            west = [source[h, pl.ds(at + width * i - 1, GROUP), :] for i in range(count)]
            yield [combine(f[i], value[i + 1], value[i + 2], value[i], east[i], west[i]) for i in range(count)]

    def substep(source, target, step):
        def some_rows(r, count):
            for t in range(width // GROUP):
                at = pl.multiple_of(start_of(r) + GROUP * t, GROUP)
                f = [weights(at - GROUP + width * i) for i in range(count)]
                for h, out in enumerate(advanced(source, at, f)):
                    for i in range(count):
                        target[h, pl.ds(at + width * i, GROUP), :] = out[i]

        def block(p, carry):
            some_rows(step + TALL * p, TALL)
            return carry

        count = rows + 2 * (HALO - step)
        lax.fori_loop(0, count // TALL, block, 0)
        if count % TALL:
            some_rows(step + count // TALL * TALL, count % TALL)

    buffers = [first, second]
    for step in range(1, SUBSTEPS):
        substep(buffers[(step - 1) % 2], buffers[step % 2], step)
    source = buffers[(SUBSTEPS - 1) % 2]
    chunk = lines

    def finish_chunk(q):
        for p in range(chunk // TALL):
            r = q * chunk + TALL * p
            for t in range(0, lanes // GROUP, 2):
                parts = []
                for u in range(2):
                    at = start_of(HALO + r) + HALO + GROUP * (t + u)
                    f = [weights(at - GROUP + width * i) for i in range(TALL)]
                    parts.append(list(advanced(source, at, f)))
                for i in range(TALL):
                    for h in range(halves):
                        both = jnp.concatenate([parts[0][h][i], parts[1][h][i]], axis=0).astype(BF16)
                        evolved[r + i, GROUP * t:GROUP * (t + 2), LANES * h:LANES * (h + 1)] = both

    def product(q):
        part = evolved[pl.ds(q * chunk, chunk)].reshape(chunk * lanes, fields)
        return lax.dot_general(part, part, (((0,), (0,)), ((), ())), preferred_element_type=F32)

    finish_chunk(0)
    gram[...] = jnp.zeros_like(gram)

    def last_chunk(q, carry):
        storing(q - 1).start()
        gram[...] += product(q - 1)
        finish_chunk(q)
        return carry

    lax.fori_loop(1, chunks, last_chunk, 0)
    storing(chunks - 1).start()
    gram[...] += product(chunks - 1)
    h = fields // 2
    ri = lax.broadcasted_iota(jnp.int32, (h, h), 0)
    ci = lax.broadcasted_iota(jnp.int32, (h, h), 1)
    corner = gram[0:h, 0:h]
    payload[0:h] = jnp.where(ri <= ci, gram[h:2 * h, h:2 * h], corner)
    payload[h:2 * h] = gram[0:h, h:2 * h]
    diagonal = jnp.sum(jnp.where(ri == ci, corner, 0.0), axis=0, keepdims=True)
    payload[2 * h:] = jnp.broadcast_to(diagonal, (PACKED, h))
    for q in range(chunks):
        storing(q).wait()


def evolve(own, low, high, sides, table):
    rows, lanes, fields = own.shape
    width = lanes + 2 * HALO
    state = (fields // LANES, (rows + 2 * HALO) * width + 2 * GROUP, LANES)
    chunks = 8
    hbm, vmem = pl.BlockSpec(memory_space=pltpu.HBM), pl.BlockSpec(memory_space=pltpu.VMEM)
    return pl.pallas_call(
        evolve_kernel,
        in_specs=[hbm, vmem, vmem, vmem, vmem],
        out_specs=(hbm, vmem),
        out_shape=(
            pltpu.HBM((rows, lanes, fields), BF16),
            jax.ShapeDtypeStruct((fields + PACKED, fields // 2), F32),
        ),
        scratch_shapes=[
            pltpu.VMEM(state, F32),
            pltpu.VMEM(state, F32),
            pltpu.VMEM((3, table.shape[1] * LANES, LANES), F32),
            pltpu.VMEM((fields, fields), F32),
            pltpu.VMEM((rows, lanes, fields), BF16),
            pltpu.SemaphoreType.DMA((chunks,)),
            pltpu.SemaphoreType.DMA((chunks,)),
        ],
        compiler_params=pltpu.CompilerParams(vmem_limit_bytes=42 << 20),
    )(pltpu.with_memory_space_constraint(own, pltpu.HBM), low, high, sides, table)


def finish_kernel(total, pay, source, factor, exponents, basis, v, held, inverse, evolved, wide, out, read, write):
    rows, lanes, fields = evolved.shape
    chunks, step = out.shape[0], out.shape[2]
    pitch = step + 1

    def loading(q):
        return pltpu.make_async_copy(source.at[pl.ds(q * step, step)], evolved.at[pl.ds(q * step, step)], read.at[q])

    def storing(q):
        return pltpu.make_async_copy(out.at[q], basis.at[:, pl.ds(q * step, step)], write.at[q])

    for q in range(chunks):
        loading(q).start()
    factor_kernel(total, pay, factor, inverse, exponents, v, held)
    for q in range(chunks):
        loading(q).wait()
        for r in range(0, step, 2):
            cells = evolved[q * step + r:q * step + r + 2].reshape(2 * lanes, fields)
            part = lax.dot_general(inverse[...], cells, (((1,), (1,)), ((), ())), preferred_element_type=F32)
            for i in range(2):
                wide[pl.ds(r + i, fields, stride=pitch), :] = part[:, i * lanes:(i + 1) * lanes]

        def narrow(f, carry):
            out[q, f] = wide[pl.ds(f * pitch, step), :].astype(BF16)
            return carry

        lax.fori_loop(0, fields, narrow, 0, unroll=64)
        storing(q).start()
    for q in range(chunks):
        storing(q).wait()


def finish(pay, evolved, total):
    rows, lanes, fields = evolved.shape
    step = 16
    chunks = rows // step
    hbm, vmem = pl.BlockSpec(memory_space=pltpu.HBM), pl.BlockSpec(memory_space=pltpu.VMEM)
    return pl.pallas_call(
        functools.partial(finish_kernel, total),
        in_specs=[vmem, hbm],
        out_specs=(vmem, vmem, hbm),
        out_shape=(
            jax.ShapeDtypeStruct((fields, fields), F32),
            jax.ShapeDtypeStruct((1, fields), F32),
            jax.ShapeDtypeStruct((fields, rows, lanes), BF16),
        ),
        scratch_shapes=[
            pltpu.VMEM((3, LANES, LANES), F32),
            pltpu.VMEM((2 * GROUP * GROUP, LANES), F32),
            pltpu.VMEM((fields, fields), BF16),
            pltpu.VMEM((rows, lanes, fields), BF16),
            pltpu.VMEM(((step + 1) * fields, lanes), F32),
            pltpu.VMEM((chunks, fields, step, lanes), BF16),
            pltpu.SemaphoreType.DMA((chunks,)),
            pltpu.SemaphoreType.DMA((chunks,)),
        ],
        compiler_params=pltpu.CompilerParams(vmem_limit_bytes=24 << 20),
    )(pay, pltpu.with_memory_space_constraint(evolved, pltpu.HBM))


def shifted(block, down, right):
    nx, ny = lax.axis_size("gx"), lax.axis_size("gy")
    pairs = []
    for x in range(nx):
        for y in range(ny):
            pairs.append((x * ny + y, (x + down) % nx * ny + (y + right) % ny))
    return lax.ppermute(block, ("gx", "gy"), pairs)


def swapped(block, axis, bit):
    return lax.ppermute(block, axis, [(i, i ^ bit) for i in range(lax.axis_size(axis))])


def summed(payload):
    nx, ny = lax.axis_size("gx"), lax.axis_size("gy")
    if nx & (nx - 1) or ny & (ny - 1) or nx < 2:
        return lax.psum(payload, ("gx", "gy"))
    half = payload.shape[0] // 2
    side = lax.axis_index("gx") % 2
    kept = lax.dynamic_slice_in_dim(payload, side * half, half, 0)
    given = lax.dynamic_slice_in_dim(payload, (1 - side) * half, half, 0)
    total = kept + swapped(given, "gx", 1)
    for axis, bits in (("gy", range(ny.bit_length() - 1)), ("gx", range(1, nx.bit_length() - 1))):
        for bit in bits:
            total = total + swapped(total, axis, 1 << bit)
    other = swapped(total, "gx", 1)
    return jnp.where(side == 0, jnp.concatenate([total, other]), jnp.concatenate([other, total]))


def pieces(block):
    out = []
    for _ in range(3):
        part = lax.reduce_precision(block, 8, 7)
        out.append(part.astype(BF16))
        block = block - part
    return jnp.concatenate(out)


def joined(parts):
    count = parts.shape[0] // 3
    wide = parts.astype(F32)
    return wide[:count] + wide[count:2 * count] + wide[2 * count:]


def tail_of(parts, fields):
    flat = parts.reshape(-1)
    return jnp.pad(flat, (0, -flat.size % (PACKED * fields))).reshape(-1, fields)


def unloaded(matrix, rows, cols):
    cells = rows * cols
    parts = matrix[cells:].reshape(-1)[:9 * cells].reshape(9, rows, cols)
    return matrix[:cells].reshape(rows, cols, -1), parts


def per_device(tangent, courant_x, courant_y, growth):
    fields, rows, cols = tangent.shape
    nx, ny = lax.axis_size("gx"), lax.axis_size("gy")
    block = jnp.stack([courant_x, courant_y, growth])
    parts = pieces(block)

    def edges(x, axis):
        size = x.shape[axis]
        return lax.slice_in_dim(x, size - HALO, size, axis=axis), lax.slice_in_dim(x, 0, HALO, axis=axis)

    part_last, part_begin = edges(parts, 1)
    part_side = jnp.concatenate(edges(parts, 2), axis=2)
    own, last, begin, both = turn(tangent, [tail_of(part, fields) for part in (part_last, part_begin, part_side)])
    low = unloaded(shifted(last, 1, 0), HALO, cols)
    high = unloaded(shifted(begin, -1, 0), HALO, cols)
    side, side_part = unloaded(shifted(both, 0, 1), rows, 2 * HALO)
    if ny > 2:
        east, east_part = unloaded(shifted(both, 0, -1), rows, 2 * HALO)
        side = jnp.concatenate([side[:, :HALO], east[:, HALO:]], axis=1)
        side_part = jnp.concatenate([side_part[:, :, :HALO], east_part[:, :, HALO:]], axis=2)

    def corner(state, part, down):
        matrix = jnp.concatenate([state.reshape(-1, fields), tail_of(part, fields)])
        return unloaded(shifted(matrix, down, 0), HALO, 2 * HALO)

    state_last, state_begin = edges(side, 0)
    part_last, part_begin = edges(side_part, 1)
    low_side = corner(state_last, part_last, 1)
    high_side = corner(state_begin, part_begin, -1)
    sides = jnp.concatenate([low_side[0], side, high_side[0]])
    middle = jnp.concatenate([joined(low[1]), block, joined(high[1])], axis=1)
    around = joined(jnp.concatenate([low_side[1], side_part, high_side[1]], axis=1))
    table = jnp.concatenate([around[:, :, :HALO], middle, around[:, :, HALO:]], axis=2)
    table = table.reshape(3, -1)
    table = jnp.pad(table, ((0, 0), (0, -table.shape[1] % LANES))).reshape(3, -1, LANES)
    evolved, payload = evolve(own, low[0], high[0], sides, table)
    total = float(rows * nx * cols * ny)
    factor, exponents, basis = finish(summed(payload), evolved, total)
    return basis, factor, exponents.reshape(fields)


def solution(mesh):
    placed = (P(None, "gx", "gy"), P("gx", "gy"), P("gx", "gy"), P("gx", "gy"))
    return jax.shard_map(
        per_device,
        mesh=mesh,
        in_specs=placed,
        out_specs=(P(None, "gx", "gy"), P(), P()),
        check_vma=False,
    )
```
